128 devices in a mesh: dp: 8 (over z, core), seq: 16 (over x, y).
Axes of the slice: x: 4, y: 4, z: 4, core: 2. Of those that a mesh axis runs over, the one named last changes fastest.
Arguments:
- queries: bfloat16 [16384, 4096], P(('dp', 'seq')), may hold values from -6 to 6
- keys: bfloat16 [16384, 512], P(('dp', 'seq')), may hold values from -6 to 6
- values: bfloat16 [16384, 512], P(('dp', 'seq')), may hold values from -6 to 6
- grad_out: bfloat16 [16384, 4096], P(('dp', 'seq')), may hold values from -6 to 6
- doc_lengths: int32 [32], replicated, may hold values from 1 to 2048, 16384 in all
Outputs:
- grad_q: bfloat16 [16384, 4096], P(('dp', 'seq'))
- grad_k: bfloat16 [16384, 512], P(('dp', 'seq'))
- grad_v: bfloat16 [16384, 512], P(('dp', 'seq'))
The draws below stay inside these ranges and needn't reach their ends.
Inputs may be any that keep to these rules, and one draw needn't show every extreme that they name: `doc_lengths`: the 32 lengths sum to 16384; the longest is exactly 2048.
All inputs are finite; a program needn't handle non-finite values.
Results may differ from the reference program's by a relative error of at most 0.0071.
Values may be sent and summed in bfloat16 or wider, within the bound.
A program may use at most 64 MiB of HBM per device.

```python
import math
import jax
import jax.numpy as jnp
import numpy as np
from jax import lax

QH = 32
KVH = 4
HD = 128
TOK_DEV = 128
GROUP_TOK = 2048
TOKENS = 16384
DOCS = 32
N_DP = 8
N_SEQ = 16


def draw_queries(key, part):
    own_key = jax.random.fold_in(key, 11)
    result = jnp.clip(jax.random.normal(own_key, (TOKENS, QH * HD), jnp.float32), -6.0, 6.0)
    return result.astype(jnp.bfloat16)


def draw_keys(key, part):
    own_key = jax.random.fold_in(key, 12)
    result = jnp.clip(jax.random.normal(own_key, (TOKENS, KVH * HD), jnp.float32), -6.0, 6.0)
    return result.astype(jnp.bfloat16)


def levels(key, extent, cuts, low, largest):
    loudness = 1.0
    for position, parts in cuts:
        steps = jax.random.uniform(jax.random.fold_in(jax.random.fold_in(key, 6), position), (parts,), jnp.float32, low / len(cuts), largest / len(cuts))
        loudness = loudness * jnp.repeat(jnp.exp(steps), extent[position] // parts).reshape((-1,) + (1,) * (len(extent) - 1 - position))
    return loudness


def split_up(count, total, bound, skew):
    portions = [(1 << 20) // math.isqrt(standing ** skew) + 1 for standing in range(2, count + 1)]
    rest, holding = total - bound - (count - 1), [1] * (count - 1)
    while rest > 0:
        movable = [i for i in range(count - 1) if holding[i] < bound]
        pool, budget = sum([portions[i] for i in movable]), rest
        for i in movable:
            more = min(bound - holding[i], max(1, budget * portions[i] // pool), rest)
            holding[i] = holding[i] + more
            rest = rest - more
    return np.array([bound] + holding)


def uneven_parts(rng, count, total, limit, lean):
    if count == 2:
        one = jax.random.randint(rng, (), max(1, total - limit), min(limit, total - 1) + 1)
        return jnp.stack([one, total - one])
    tallies = jnp.asarray(split_up(count, total, limit, lean), jnp.int32)
    twos = (count - 1) // 2
    source_of, receiver = tallies[1:1 + 2 * twos:2], tallies[2:2 + 2 * twos:2]
    slack = jnp.minimum(source_of - 1, limit - receiver)
    shifted = jax.random.randint(jax.random.fold_in(rng, 1), (twos,), 0, 1 << 20) % (slack + 1)
    tallies = tallies.at[1:1 + 2 * twos:2].set(source_of - shifted).at[2:2 + 2 * twos:2].set(receiver + shifted)
    return tallies[jax.random.permutation(jax.random.fold_in(rng, 2), count)]


def normal_values(stream_key, shape, width, bound, shards=(), held_as=jnp.bfloat16):
    values = jax.random.normal(stream_key, shape, jnp.float32) * width
    if len(shards) > 0:
        values = levels(stream_key, shape, shards, -0.22, 0.18) * values
    return jnp.clip(values, min=-bound, max=bound).astype(held_as)


def setup_inputs(seed: int = 0) -> dict:
    seeds = jax.random.split(jax.random.key(seed), 6)
    queries = draw_queries(jax.random.fold_in(seeds[5], 71), 0)
    keys = draw_keys(jax.random.fold_in(seeds[5], 71), 0)
    values = normal_values(seeds[2], (TOKENS, KVH * HD), 1.0, 6.0, ((0, 128),))
    grad_out = normal_values(seeds[3], (TOKENS, QH * HD), 1.0, 6.0, ((0, 128),))
    doc_lengths = uneven_parts(seeds[4], DOCS, TOKENS, GROUP_TOK, 2).astype(jnp.int32)
    return dict(queries=queries, keys=keys, values=values, grad_out=grad_out, doc_lengths=doc_lengths)


def doc_index(positions, doc_ends):
    inside = (positions[:, None] >= doc_ends[None, :]).astype(jnp.int32)
    return jnp.sum(inside, axis=1).astype(jnp.int32) - (positions < 0).astype(jnp.int32)


def reference(queries, keys, values, grad_out, doc_lengths):
    group_len = TOK_DEV * N_SEQ
    per_kv = QH // KVH
    inv_root = HD ** -0.5
    doc_ends = jnp.cumsum(doc_lengths).astype(jnp.int32)
    q_groups = queries.reshape(N_DP, group_len, QH, HD)
    o_groups = grad_out.reshape(N_DP, group_len, QH, HD)
    zero_rows = jnp.zeros((group_len, KVH * HD), jnp.bfloat16)
    k_padded = jnp.concatenate([zero_rows, keys], 0).reshape(N_DP + 1, group_len, KVH, HD)
    v_padded = jnp.concatenate([zero_rows, values], 0).reshape(N_DP + 1, group_len, KVH, HD)
    zero_index = jnp.zeros((), jnp.int32)

    def one_group(state_now, inputs):
        acc_k, acc_v = state_now
        grp_index, q_grp, o_grp = inputs
        grp_index = grp_index.astype(jnp.int32)
        k_window = lax.dynamic_slice_in_dim(k_padded, grp_index, 2, 0).reshape(2 * group_len, KVH, HD)
        v_window = lax.dynamic_slice_in_dim(v_padded, grp_index, 2, 0).reshape(2 * group_len, KVH, HD)
        q_pos = grp_index * group_len + jnp.arange(group_len, dtype=jnp.int32)
        k_pos = (grp_index - 1) * group_len + jnp.arange(2 * group_len, dtype=jnp.int32)
        allowed = (doc_index(q_pos, doc_ends)[:, None] == doc_index(k_pos, doc_ends)[None, :]) & (k_pos[None, :] <= q_pos[:, None])

        def per_head(pieces):
            q_head, o_head, head_idx = pieces
            kv_idx = (head_idx // per_kv).astype(jnp.int32)
            k_head = lax.dynamic_index_in_dim(k_window, kv_idx, 1, keepdims=False)
            v_head = lax.dynamic_index_in_dim(v_window, kv_idx, 1, keepdims=False)
            scores = jnp.dot(q_head, k_head.T, preferred_element_type=jnp.float32) * inv_root
            scores = jnp.where(allowed, scores, -1e30)
            row_peak = jnp.max(scores, axis=1, keepdims=True)
            log_norm = row_peak + jnp.log(jnp.sum(jnp.where(allowed, jnp.exp(scores - row_peak), 0.0), axis=1, keepdims=True))
            prob_f = jnp.where(allowed, jnp.exp(scores - log_norm), 0.0)
            dprobs = jnp.dot(o_head, v_head.T, preferred_element_type=jnp.float32)
            row_delta = jnp.sum(prob_f * dprobs, axis=1, keepdims=True)
            probs_b = prob_f.astype(jnp.bfloat16)
            dscores = (prob_f * (dprobs - row_delta)).astype(jnp.bfloat16)
            grad_qh = (jnp.dot(dscores, k_head, preferred_element_type=jnp.float32) * inv_root).astype(jnp.bfloat16)
            grad_kh = jnp.dot(dscores.T, q_head, preferred_element_type=jnp.float32) * inv_root
            grad_vh = jnp.dot(probs_b.T, o_head, preferred_element_type=jnp.float32)
            return grad_qh, grad_kh, grad_vh

        head_ids = jnp.arange(QH, dtype=jnp.int32)
        grad_qs, grad_ks, grad_vs = lax.map(per_head, (q_grp.transpose(1, 0, 2), o_grp.transpose(1, 0, 2), head_ids))
        grad_ks = grad_ks.reshape(KVH, per_kv, 2 * group_len, HD).sum(1).transpose(1, 0, 2).reshape(2, group_len, KVH, HD)
        grad_vs = grad_vs.reshape(KVH, per_kv, 2 * group_len, HD).sum(1).transpose(1, 0, 2).reshape(2, group_len, KVH, HD)
        begin_at = (grp_index, zero_index, zero_index, zero_index)
        acc_k = lax.dynamic_update_slice(acc_k, lax.dynamic_slice(acc_k, begin_at, (2, group_len, KVH, HD)) + grad_ks, begin_at)
        acc_v = lax.dynamic_update_slice(acc_v, lax.dynamic_slice(acc_v, begin_at, (2, group_len, KVH, HD)) + grad_vs, begin_at)
        return (acc_k, acc_v), grad_qs.transpose(1, 0, 2)

    start_acc = jnp.zeros((N_DP + 1, group_len, KVH, HD), jnp.float32)
    group_ids = jnp.arange(N_DP, dtype=jnp.int32)
    (acc_k, acc_v), grad_q = lax.scan(one_group, (start_acc, start_acc), (group_ids, q_groups, o_groups))
    grad_q = grad_q.reshape(TOKENS, QH * HD)
    grad_k = acc_k[1:].reshape(TOKENS, KVH * HD).astype(jnp.bfloat16)
    grad_v = acc_v[1:].reshape(TOKENS, KVH * HD).astype(jnp.bfloat16)
    return grad_q, grad_k, grad_v
```

```python
import functools

import jax
import jax.numpy as jnp
from jax import lax
from jax.experimental import pallas as pl
from jax.experimental.pallas import tpu as pltpu
from jax.sharding import PartitionSpec as P

MESH = pl.DeviceIdType.MESH
SIDE = 4
TOK = 128
HD = 128
GW = 1024
PER_KV = GW // HD
GROUP = SIDE * SIDE * TOK
WIN = 2 * GROUP
KB = 256
STEPS = 9
LOG2E = 1.4426950408889634
INV_ROOT = HD ** -0.5
LOW = -1e30


def place():
    seq = lax.axis_index("seq")
    return lax.axis_index("dp"), lax.div(seq, SIDE), lax.rem(seq, SIDE)


def greet(dp, x, y):
    barrier = pltpu.get_barrier_semaphore()
    count = lax.axis_size("dp")
    peers = [{"seq": lax.rem(x + d, SIDE) * SIDE + y} for d in range(1, SIDE)]
    peers += [{"seq": x * SIDE + lax.rem(y + d, SIDE)} for d in range(1, SIDE)]
    peers += [{"dp": lax.rem(dp + 1, count)}, {"dp": lax.rem(dp + count - 1, count)}]
    for peer in peers:
        pl.semaphore_signal(barrier, inc=1, device_id=peer, device_id_type=MESH)
    pl.semaphore_wait(barrier, len(peers))


def cols(index, width):
    return pl.ds(pl.multiple_of(index * width, width), width)


def gather_kernel(q, o, k, v, qo, kv, relay, send, recv, here):
    dp, x, y = place()
    count = lax.axis_size("dp")
    used = [0]

    def remote(src, dst, device):
        i = used[0]
        used[0] += 1
        copy = pltpu.make_async_remote_copy(
            src_ref=src, dst_ref=dst, send_sem=send.at[i], recv_sem=recv.at[i],
            device_id=device, device_id_type=MESH,
        )
        copy.start()
        return copy

    def local(src, dst, i):
        copy = pltpu.make_async_copy(src, dst, here.at[i])
        copy.start()
        return copy

    def at_x(d):
        return {"seq": lax.rem(x + d, SIDE) * SIDE + y}

    def at_y(d):
        return {"seq": x * SIDE + lax.rem(y + d, SIDE)}

    greet(dp, x, y)
    locals_kv = [local(a.at[:, cols(x, HD)], kv.at[n, 1, x, y], n) for n, a in enumerate((k, v))]
    first = []
    for d in (1, 3, 2):
        head = lax.rem(x + d, SIDE)
        for n, a in enumerate((k, v)):
            first.append(remote(a.at[:, cols(head, HD)], kv.at[n, 1, x, y], at_x(d)))
    far = lax.rem(x + 2, SIDE)
    half = TOK // 2
    passing = []
    for n, a in enumerate((q, o)):
        passing.append(remote(a.at[pl.ds(0, half), cols(far, GW)], relay.at[n, 0], at_x(1)))
        passing.append(remote(a.at[pl.ds(half, half), cols(far, GW)], relay.at[n, 1], at_x(3)))
    direct = []
    for n, a in enumerate((q, o)):
        for d in (1, 3):
            head = lax.rem(x + d, SIDE)
            direct.append(remote(a.at[:, cols(head, GW)], qo.at[n, x], at_x(d)))
    locals_q = [local(a.at[:, cols(x, GW)], qo.at[n, x], 2 + n) for n, a in enumerate((q, o))]
    for copy in locals_kv:
        copy.wait()
    for copy in first:
        copy.wait_recv()
    mine = kv.at[:, 1, :, y]
    after = {"dp": lax.rem(dp + 1, count)}
    along = [remote(mine, mine, at_y(d)) for d in (1, 3, 2)]
    later = [remote(mine, kv.at[:, 0, :, y], after)]
    onward = []
    for n in range(2):
        passing[2 * n].wait_recv()
        origin = lax.rem(x + 3, SIDE)
        onward.append(remote(relay.at[n, 0], qo.at[n, origin, pl.ds(0, half)], at_x(1)))
        passing[2 * n + 1].wait_recv()
        origin = lax.rem(x + 1, SIDE)
        onward.append(remote(relay.at[n, 1], qo.at[n, origin, pl.ds(half, half)], at_x(3)))
    for copy, d in zip(along, (1, 3, 2)):
        copy.wait_recv()
        source = lax.rem(y + SIDE - d, SIDE)
        later.append(remote(kv.at[:, 1, :, source], kv.at[:, 0, :, source], after))
    for copy in direct + onward + later:
        copy.wait_recv()
    for copy in locals_q:
        copy.wait()
    for copy in first + passing + direct + along + onward + later:
        copy.wait_send()


GATHER_COPIES = 6 + 4 + 4 + 3 + 4 + 4


def gather(queries, grad_out, keys, values):
    return pl.pallas_call(
        gather_kernel,
        out_shape=(
            jax.ShapeDtypeStruct((2, SIDE, TOK, GW), jnp.bfloat16),
            jax.ShapeDtypeStruct((2, 2, SIDE, SIDE, TOK, HD), jnp.bfloat16),
        ),
        in_specs=[pl.BlockSpec(memory_space=pltpu.VMEM)] * 4,
        out_specs=(pl.BlockSpec(memory_space=pltpu.VMEM),) * 2,
        scratch_shapes=[
            pltpu.VMEM((2, 2, TOK // 2, GW), jnp.bfloat16),
            pltpu.SemaphoreType.DMA((GATHER_COPIES,)),
            pltpu.SemaphoreType.DMA((GATHER_COPIES,)),
            pltpu.SemaphoreType.DMA((4,)),
        ],
        compiler_params=pltpu.CompilerParams(collective_id=0, has_side_effects=True),
        name="gather",
    )(queries, grad_out, keys, values)


def return_kernel(gq, dkv, out_q, out_k, out_v, relay, z_in, y_out, y_in, x_out, send, recv, here):
    dp, x, y = place()
    count = lax.axis_size("dp")
    used = [0]

    def remote(src, dst, device):
        i = used[0]
        used[0] += 1
        copy = pltpu.make_async_remote_copy(
            src_ref=src, dst_ref=dst, send_sem=send.at[i], recv_sem=recv.at[i],
            device_id=device, device_id_type=MESH,
        )
        copy.start()
        return copy

    def at_x(d):
        return {"seq": lax.rem(x + d, SIDE) * SIDE + y}

    def at_y(d):
        return {"seq": x * SIDE + lax.rem(y + d, SIDE)}

    greet(dp, x, y)
    before = {"dp": lax.rem(dp + count - 1, count)}
    order = (2, 1, 3, 0)
    down = {d: remote(dkv.at[:, 0, :, lax.rem(y + d, SIDE)], z_in.at[d], before) for d in order}
    half = TOK // 2
    far = lax.rem(x + 2, SIDE)
    passing = [
        remote(gq.at[far, pl.ds(0, half)], relay.at[0], at_x(1)),
        remote(gq.at[far, pl.ds(half, half)], relay.at[1], at_x(3)),
    ]
    direct = [remote(gq.at[lax.rem(x + d, SIDE)], out_q.at[:, cols(x, GW)], at_x(d)) for d in (1, 3)]
    own = pltpu.make_async_copy(gq.at[x], out_q.at[:, cols(x, GW)], here.at[0])
    own.start()

    def total(d):
        down[d].wait_recv()
        part = dkv[:, 1, :, lax.rem(y + d, SIDE)].astype(jnp.float32)
        return part + z_in[d].astype(jnp.float32)

    across = {}
    onward = []
    for d in order[:3]:
        y_out[d - 1] = total(d).astype(jnp.bfloat16)
        across[d] = remote(y_out.at[d - 1], y_in.at[d - 1], at_y(d))
        if d == 2:
            passing[0].wait_recv()
            origin = lax.rem(x + 3, SIDE)
            onward.append(remote(relay.at[0], out_q.at[pl.ds(0, half), cols(origin, GW)], at_x(1)))
            passing[1].wait_recv()
            origin = lax.rem(x + 1, SIDE)
            onward.append(remote(relay.at[1], out_q.at[pl.ds(half, half), cols(origin, GW)], at_x(3)))
    mine = total(0)
    for d in order[:3]:
        across[d].wait_recv()
        mine = mine + y_in[d - 1].astype(jnp.float32)
    x_out[...] = mine.astype(jnp.bfloat16)
    back = []
    for d in (2, 1, 3):
        target = lax.rem(x + d, SIDE)
        for n, out in enumerate((out_k, out_v)):
            back.append(remote(x_out.at[n, target], out.at[:, cols(x, HD)], at_x(d)))
    for n, out in enumerate((out_k, out_v)):
        out[:, cols(x, HD)] = x_out[n, x]
    for copy in direct + onward + back:
        copy.wait_recv()
    own.wait()
    for copy in list(down.values()) + passing + direct + list(across.values()) + onward + back:
        copy.wait_send()


RETURN_COPIES = 4 + 2 + 2 + 3 + 2 + 6


def give_back(gq, dkv):
    piece = (2, SIDE, TOK, HD)
    return pl.pallas_call(
        return_kernel,
        out_shape=(
            jax.ShapeDtypeStruct((TOK, SIDE * GW), jnp.bfloat16),
            jax.ShapeDtypeStruct((TOK, SIDE * HD), jnp.bfloat16),
            jax.ShapeDtypeStruct((TOK, SIDE * HD), jnp.bfloat16),
        ),
        in_specs=[pl.BlockSpec(memory_space=pltpu.VMEM)] * 2,
        out_specs=(pl.BlockSpec(memory_space=pltpu.VMEM),) * 3,
        scratch_shapes=[
            pltpu.VMEM((2, TOK // 2, GW), jnp.bfloat16),
            pltpu.VMEM((4,) + piece, jnp.bfloat16),
            pltpu.VMEM((3,) + piece, jnp.bfloat16),
            pltpu.VMEM((3,) + piece, jnp.bfloat16),
            pltpu.VMEM(piece, jnp.bfloat16),
            pltpu.SemaphoreType.DMA((RETURN_COPIES,)),
            pltpu.SemaphoreType.DMA((RETURN_COPIES,)),
            pltpu.SemaphoreType.DMA((1,)),
        ],
        compiler_params=pltpu.CompilerParams(collective_id=1, has_side_effects=True),
        name="give_back",
    )(gq, dkv)


def fold(tile):
    return tile.reshape(KB // 8, 8, HD)


def attend_kernel(place_ref, lens, qo, kv, gq, dkv, qs, os, s_buf, dp_buf, dq, acc_k, acc_v, top, norm, dots):
    group, y = place_ref[0], place_ref[1]
    first_key = (group - 1) * GROUP
    acc_k[...] = jnp.zeros_like(acc_k)
    acc_v[...] = jnp.zeros_like(acc_v)
    nt = (((1,), (1,)), ((), ()))
    tn = (((0,), (0,)), ((), ()))

    def dot(a, b, dims):
        return lax.dot_general(a, b, dims, preferred_element_type=jnp.float32)

    def heads():
        return [(h, slice(h * HD, (h + 1) * HD)) for h in range(PER_KV)]

    @pl.loop(0, SIDE)
    def _(row):
        for h, span in heads():
            qs[span, :] = qo[0, row, :, span]
            os[span, :] = qo[1, row, :, span]
        block = row * SIDE + y
        head_pos = group * GROUP + block * TOK
        pos = head_pos + lax.broadcasted_iota(jnp.int32, (8, TOK), 1)

        def one_doc(i, state):
            end, low, lows = state
            end = end + lens[i]
            low = jnp.where(end <= head_pos, end, low)
            lows = jnp.where(end <= pos, end, lows)
            return end, low, lows

        zero = jnp.int32(0)
        _, low, lows = lax.fori_loop(
            0, lens.shape[0], one_doc, (zero, zero, jnp.zeros((8, TOK), jnp.int32))
        )
        low_block = lax.div(low - first_key, TOK)
        end_block = GROUP // TOK + block + 1
        steps = lax.div(end_block - low_block + 1, 2)
        base = jnp.maximum(0, end_block - 2 * steps) * TOK
        lows_b = jnp.broadcast_to(lows[0:1], (KB, TOK)) - first_key
        pos_b = jnp.broadcast_to(pos[0:1], (KB, TOK)) - first_key

        def keys_of(j):
            return pl.ds(pl.multiple_of(base + j * KB, TOK), KB)

        top[...] = jnp.full_like(top, LOW)
        norm[...] = jnp.zeros_like(norm)
        dots[...] = jnp.zeros_like(dots)
        dq[...] = jnp.zeros_like(dq)

        @pl.loop(0, steps)
        def _(j):
            scores = dot(kv[0, keys_of(j), :], qs[...], nt)
            key = base + j * KB + lax.broadcasted_iota(jnp.int32, (KB, TOK), 0)
            allowed = (key >= lows_b) & (key <= pos_b)
            for h, span in heads():
                tile = jnp.where(allowed, scores[:, span], LOW)
                s_buf[j, :, span] = tile
                top[:, span] = jnp.maximum(top[:, span], jnp.max(fold(tile), axis=0))

        peak = jnp.max(top[...], axis=0, keepdims=True) * (INV_ROOT * LOG2E)
        top[...] = jnp.broadcast_to(peak, top.shape)

        @pl.loop(0, steps)
        def _(j):
            dprobs = dot(kv[1, keys_of(j), :], os[...], nt)
            for h, span in heads():
                shift = jnp.broadcast_to(top[0:1, span], (KB, TOK))
                weight = jnp.exp2(s_buf[j, :, span] * (INV_ROOT * LOG2E) - shift)
                dprob = dprobs[:, span]
                s_buf[j, :, span] = weight
                dp_buf[j, :, span] = dprob
                norm[:, span] += jnp.sum(fold(weight), axis=0)
                dots[:, span] += jnp.sum(fold(weight * dprob), axis=0)

        inv = 1.0 / jnp.sum(norm[...], axis=0, keepdims=True)
        delta = jnp.sum(dots[...], axis=0, keepdims=True) * inv
        norm[...] = jnp.broadcast_to(inv, norm.shape)
        dots[...] = jnp.broadcast_to(delta, dots.shape)

        @pl.loop(0, steps)
        def _(j):
            probs, dscores = [], []
            for h, span in heads():
                prob = s_buf[j, :, span] * jnp.broadcast_to(norm[0:1, span], (KB, TOK))
                minus = jnp.broadcast_to(dots[0:1, span], (KB, TOK))
                probs.append(prob.astype(jnp.bfloat16))
                dscores.append((prob * (dp_buf[j, :, span] - minus)).astype(jnp.bfloat16))
            probs = jnp.concatenate(probs, axis=1)
            dscores = jnp.concatenate(dscores, axis=1)
            nn = (((1,), (0,)), ((), ()))
            acc_v[keys_of(j), :] += dot(probs, os[...], nn)
            acc_k[keys_of(j), :] += dot(dscores, qs[...], nn)
            dq[...] += dot(kv[0, keys_of(j), :], dscores, tn)

        for h, span in heads():
            gq[row, :, span] = (dq[:, span].T * INV_ROOT).astype(jnp.bfloat16)

    dkv[0] = (acc_k[...] * INV_ROOT).astype(jnp.bfloat16)
    dkv[1] = acc_v[...].astype(jnp.bfloat16)


def attend(where, doc_lengths, qo, kv):
    rows = PER_KV * TOK
    vmem = pl.BlockSpec(memory_space=pltpu.VMEM)
    smem = pl.BlockSpec(memory_space=pltpu.SMEM)
    return pl.pallas_call(
        attend_kernel,
        out_shape=(
            jax.ShapeDtypeStruct((SIDE, TOK, GW), jnp.bfloat16),
            jax.ShapeDtypeStruct((2, WIN, HD), jnp.bfloat16),
        ),
        in_specs=[smem, smem, vmem, vmem],
        out_specs=(vmem, vmem),
        scratch_shapes=[
            pltpu.VMEM((rows, HD), jnp.bfloat16),
            pltpu.VMEM((rows, HD), jnp.bfloat16),
            pltpu.VMEM((STEPS, KB, rows), jnp.float32),
            pltpu.VMEM((STEPS, KB, rows), jnp.float32),
            pltpu.VMEM((HD, rows), jnp.float32),
            pltpu.VMEM((WIN, HD), jnp.float32),
            pltpu.VMEM((WIN, HD), jnp.float32),
            pltpu.VMEM((8, rows), jnp.float32),
            pltpu.VMEM((8, rows), jnp.float32),
            pltpu.VMEM((8, rows), jnp.float32),
        ],
        compiler_params=pltpu.CompilerParams(vmem_limit_bytes=52 * 1024 * 1024),
        name="attend",
    )(where, doc_lengths, qo, kv)


def local(queries, keys, values, grad_out, doc_lengths):
    qo, kv = gather(queries, grad_out, keys, values)
    where = jnp.stack([lax.axis_index("dp"), lax.rem(lax.axis_index("seq"), SIDE)]).astype(jnp.int32)
    gq, dkv = attend(where, doc_lengths, qo, kv.reshape(2, WIN, HD))
    return give_back(gq, dkv.reshape(2, 2, SIDE, SIDE, TOK, HD))


def solution(mesh):
    split = P(("dp", "seq"), None)
    return jax.shard_map(
        local,
        mesh=mesh,
        in_specs=(split, split, split, split, P()),
        out_specs=(split, split, split),
        check_vma=False,
    )
```

```python
import functools

import jax
import jax.numpy as jnp
from jax import lax
from jax.experimental import pallas as pl
from jax.experimental.pallas import tpu as pltpu
from jax.sharding import PartitionSpec as P

MESH = pl.DeviceIdType.MESH
SIDE = 4
TOK = 128
HD = 128
GW = 1024
PER_KV = GW // HD
GROUP = SIDE * SIDE * TOK
WIN = 2 * GROUP
KB = 256
STEPS = 9
LOG2E = 1.4426950408889634
INV_ROOT = HD ** -0.5
LOW = -1e30
SCALE2 = INV_ROOT * LOG2E


def place():
    seq = lax.axis_index("seq")
    return lax.axis_index("dp"), lax.div(seq, SIDE), lax.rem(seq, SIDE)


def greet(dp, x, y):
    barrier = pltpu.get_barrier_semaphore()
    count = lax.axis_size("dp")
    peers = [{"seq": lax.rem(x + d, SIDE) * SIDE + y} for d in range(1, SIDE)]
    peers += [{"seq": x * SIDE + lax.rem(y + d, SIDE)} for d in range(1, SIDE)]
    peers += [{"dp": lax.rem(dp + 1, count)}, {"dp": lax.rem(dp + count - 1, count)}]
    for peer in peers:
        pl.semaphore_signal(barrier, inc=1, device_id=peer, device_id_type=MESH)
    pl.semaphore_wait(barrier, len(peers))


def cols(index, width):
    return pl.ds(pl.multiple_of(index * width, width), width)


def gather_kernel(q, o, k, v, qo, kv, own_qo, own_kv, send, recv, here):
    dp, x, y = place()
    count = lax.axis_size("dp")
    used = [0]

    def remote(src, dst, device):
        i = used[0]
        used[0] += 1
        copy = pltpu.make_async_remote_copy(
            src_ref=src, dst_ref=dst, send_sem=send.at[i], recv_sem=recv.at[i],
            device_id=device, device_id_type=MESH,
        )
        copy.start()
        return copy

    def at_x(d):
        return {"seq": lax.rem(x + d, SIDE) * SIDE + y}

    def at_y(d):
        return {"seq": x * SIDE + lax.rem(y + d, SIDE)}

    def there(src, stage, i):
        copy = pltpu.make_async_copy(src, stage, here.at[i])
        copy.start()
        return copy

    stages = [
        there(a.at[:, cols(x, HD)], own_kv.at[n], n) for n, a in enumerate((k, v))
    ] + [there(a.at[:, cols(x, GW)], own_qo.at[n], 2 + n) for n, a in enumerate((q, o))]
    greet(dp, x, y)
    first = []
    for d in (1, 3, 2):
        head = lax.rem(x + d, SIDE)
        for n, a in enumerate((k, v)):
            first.append(remote(a.at[:, cols(head, HD)], kv.at[n, 1, x, y], at_x(d)))
    direct = []
    for n, a in enumerate((q, o)):
        for d in (2, 1, 3):
            head = lax.rem(x + d, SIDE)
            direct.append(remote(a.at[:, cols(head, GW)], qo.at[n, x], at_x(d)))
    for copy in stages:
        copy.wait()
    puts = [there(own_kv, kv.at[:, 1, x, y], 4), there(own_qo, qo.at[:, x], 5)]
    for copy in first:
        copy.wait_recv()
    puts[0].wait()
    mine = kv.at[:, 1, :, y]
    after = {"dp": lax.rem(dp + 1, count)}
    along = [remote(mine, mine, at_y(d)) for d in (2, 1, 3)]
    later = [remote(mine, kv.at[:, 0, :, y], after)]
    for copy, d in zip(along[1:] + along[:1], (1, 3, 2)):
        copy.wait_recv()
        source = lax.rem(y + SIDE - d, SIDE)
        later.append(remote(kv.at[:, 1, :, source], kv.at[:, 0, :, source], after))
    for copy in direct + later:
        copy.wait_recv()
    puts[1].wait()
    for copy in first + direct + along + later:
        copy.wait_send()


GATHER_COPIES = 6 + 6 + 3 + 4


def gather(queries, grad_out, keys, values):
    return pl.pallas_call(
        gather_kernel,
        out_shape=(
            jax.ShapeDtypeStruct((2, SIDE, TOK, GW), jnp.bfloat16),
            jax.ShapeDtypeStruct((2, 2, SIDE, SIDE, TOK, HD), jnp.bfloat16),
        ),
        in_specs=[pl.BlockSpec(memory_space=pltpu.HBM)] * 4,
        out_specs=(pl.BlockSpec(memory_space=pl.ANY),) * 2,
        scratch_shapes=[
            pltpu.VMEM((2, TOK, GW), jnp.bfloat16),
            pltpu.VMEM((2, TOK, HD), jnp.bfloat16),
            pltpu.SemaphoreType.DMA((GATHER_COPIES,)),
            pltpu.SemaphoreType.DMA((GATHER_COPIES,)),
            pltpu.SemaphoreType.DMA((6,)),
        ],
        compiler_params=pltpu.CompilerParams(collective_id=0, has_side_effects=True, vmem_limit_bytes=4 * 1024 * 1024),
        name="gather",
    )(queries, grad_out, keys, values)


def return_kernel(gq, dkv, out_q, out_k, out_v, relay, z_in, y_out, y_in, x_out, send, recv, here):
    dp, x, y = place()
    count = lax.axis_size("dp")
    used = [0]

    def remote(src, dst, device):
        i = used[0]
        used[0] += 1
        copy = pltpu.make_async_remote_copy(
            src_ref=src, dst_ref=dst, send_sem=send.at[i], recv_sem=recv.at[i],
            device_id=device, device_id_type=MESH,
        )
        copy.start()
        return copy

    def at_x(d):
        return {"seq": lax.rem(x + d, SIDE) * SIDE + y}

    def at_y(d):
        return {"seq": x * SIDE + lax.rem(y + d, SIDE)}

    greet(dp, x, y)
    before = {"dp": lax.rem(dp + count - 1, count)}
    order = (2, 1, 3, 0)
    down = {d: remote(dkv.at[:, 0, :, lax.rem(y + d, SIDE)], z_in.at[d], before) for d in order}
    half = TOK // 2
    far = lax.rem(x + 2, SIDE)
    passing = [
        remote(gq.at[far, pl.ds(0, half)], relay.at[0], at_x(1)),
        remote(gq.at[far, pl.ds(half, half)], relay.at[1], at_x(3)),
    ]
    direct = [remote(gq.at[lax.rem(x + d, SIDE)], out_q.at[:, cols(x, GW)], at_x(d)) for d in (1, 3)]
    own = pltpu.make_async_copy(gq.at[x], out_q.at[:, cols(x, GW)], here.at[0])
    own.start()

    def total(d):
        down[d].wait_recv()
        part = dkv[:, 1, :, lax.rem(y + d, SIDE)].astype(jnp.float32)
        return part + z_in[d].astype(jnp.float32)

    across = {}
    onward = []
    for d in order[:3]:
        y_out[d - 1] = total(d).astype(jnp.bfloat16)
        across[d] = remote(y_out.at[d - 1], y_in.at[d - 1], at_y(d))
        if d == 2:
            passing[0].wait_recv()
            origin = lax.rem(x + 3, SIDE)
            onward.append(remote(relay.at[0], out_q.at[pl.ds(0, half), cols(origin, GW)], at_x(1)))
            passing[1].wait_recv()
            origin = lax.rem(x + 1, SIDE)
            onward.append(remote(relay.at[1], out_q.at[pl.ds(half, half), cols(origin, GW)], at_x(3)))
    mine = total(0)
    for d in order[:3]:
        across[d].wait_recv()
        mine = mine + y_in[d - 1].astype(jnp.float32)
    x_out[...] = mine.astype(jnp.bfloat16)
    back = []
    for d in (2, 1, 3):
        target = lax.rem(x + d, SIDE)
        for n, out in enumerate((out_k, out_v)):
            back.append(remote(x_out.at[n, target], out.at[:, cols(x, HD)], at_x(d)))
    for n, out in enumerate((out_k, out_v)):
        out[:, cols(x, HD)] = x_out[n, x]
    for copy in direct + onward + back:
        copy.wait_recv()
    own.wait()
    for copy in list(down.values()) + passing + direct + list(across.values()) + onward + back:
        copy.wait_send()


RETURN_COPIES = 4 + 2 + 2 + 3 + 2 + 6


def give_back(gq, dkv):
    piece = (2, SIDE, TOK, HD)
    return pl.pallas_call(
        return_kernel,
        out_shape=(
            jax.ShapeDtypeStruct((TOK, SIDE * GW), jnp.bfloat16),
            jax.ShapeDtypeStruct((TOK, SIDE * HD), jnp.bfloat16),
            jax.ShapeDtypeStruct((TOK, SIDE * HD), jnp.bfloat16),
        ),
        in_specs=[pl.BlockSpec(memory_space=pltpu.VMEM)] * 2,
        out_specs=(pl.BlockSpec(memory_space=pltpu.VMEM),) * 3,
        scratch_shapes=[
            pltpu.VMEM((2, TOK // 2, GW), jnp.bfloat16),
            pltpu.VMEM((4,) + piece, jnp.bfloat16),
            pltpu.VMEM((3,) + piece, jnp.bfloat16),
            pltpu.VMEM((3,) + piece, jnp.bfloat16),
            pltpu.VMEM(piece, jnp.bfloat16),
            pltpu.SemaphoreType.DMA((RETURN_COPIES,)),
            pltpu.SemaphoreType.DMA((RETURN_COPIES,)),
            pltpu.SemaphoreType.DMA((1,)),
        ],
        compiler_params=pltpu.CompilerParams(collective_id=1, has_side_effects=True, vmem_limit_bytes=14 * 1024 * 1024),
        name="give_back",
    )(gq, dkv)


def fold(tile):
    return tile.reshape(KB // 8, 8, HD)


def attend_kernel(place_ref, lens, qo, kv, gq, dkv, qs, os, s_buf, dp_buf, dq, acc_k, acc_v, top, norm, dots):
    group, y = place_ref[0], place_ref[1]
    first_key = (group - 1) * GROUP
    acc_k[...] = jnp.zeros_like(acc_k)
    acc_v[...] = jnp.zeros_like(acc_v)
    nt = (((1,), (1,)), ((), ()))
    tn = (((0,), (0,)), ((), ()))
    nn = (((1,), (0,)), ((), ()))

    def dot(a, b, dims):
        return lax.dot_general(a, b, dims, preferred_element_type=jnp.float32)

    def heads():
        return [(h, slice(h * HD, (h + 1) * HD)) for h in range(PER_KV)]

    @pl.loop(0, SIDE)
    def _(row):
        for h, span in heads():
            qs[span, :] = qo[0, row, :, span]
            os[span, :] = qo[1, row, :, span]
        block = row * SIDE + y
        head_pos = group * GROUP + block * TOK
        pos = head_pos + lax.broadcasted_iota(jnp.int32, (8, TOK), 1)

        def one_doc(i, state):
            end, low, lows = state
            end = end + lens[i]
            low = jnp.where(end <= head_pos, end, low)
            lows = jnp.where(end <= pos, end, lows)
            return end, low, lows

        zero = jnp.int32(0)
        _, low, lows = lax.fori_loop(
            0, lens.shape[0], one_doc, (zero, zero, jnp.zeros((8, TOK), jnp.int32))
        )
        low_block = lax.div(low - first_key, TOK)
        end_block = GROUP // TOK + block + 1
        steps = lax.div(end_block - low_block + 1, 2)
        base = jnp.maximum(0, end_block - 2 * steps) * TOK
        lows_b = jnp.broadcast_to(lows[0:1], (KB, TOK)) - first_key
        pos_b = jnp.broadcast_to(pos[0:1], (KB, TOK)) - first_key

        def keys_of(j):
            return pl.ds(pl.multiple_of(base + j * KB, TOK), KB)

        top[...] = jnp.full_like(top, LOW)
        norm[...] = jnp.zeros_like(norm)
        dots[...] = jnp.zeros_like(dots)
        dq[...] = jnp.zeros_like(dq)

        @pl.loop(0, steps)
        def _(j):
            scores = dot(kv[0, keys_of(j), :], qs[...], nt)
            dprobs = dot(kv[1, keys_of(j), :], os[...], nt)
            key = base + j * KB + lax.broadcasted_iota(jnp.int32, (KB, TOK), 0)
            allowed = (key >= lows_b) & (key <= pos_b)
            for h, span in heads():
                tile = jnp.where(allowed, scores[:, span] * SCALE2, LOW)
                s_buf[j, :, span] = tile
                dprob = dprobs[:, span]
                dp_buf[j, :, span] = dprob
                old = top[:, span]
                new = jnp.maximum(old, jnp.max(fold(tile), axis=0))
                top[:, span] = new
                weight = jnp.exp2(fold(tile) - new[None])
                shrink = jnp.exp2(old - new)
                norm[:, span] = norm[:, span] * shrink + jnp.sum(weight, axis=0)
                dots[:, span] = dots[:, span] * shrink + jnp.sum(weight * fold(dprob), axis=0)

        part = top[...]
        peak = jnp.max(part, axis=0, keepdims=True)
        share = jnp.exp2(part - peak)
        total = jnp.sum(norm[...] * share, axis=0, keepdims=True)
        delta = jnp.sum(dots[...] * share, axis=0, keepdims=True) / total
        norm[...] = jnp.broadcast_to(peak + jnp.log2(total), norm.shape)
        dots[...] = jnp.broadcast_to(delta, dots.shape)

        @pl.loop(0, steps)
        def _(j):
            probs, dscores = [], []
            for h, span in heads():
                prob = jnp.exp2(fold(s_buf[j, :, span]) - norm[:, span][None])
                dscore = prob * (fold(dp_buf[j, :, span]) - dots[:, span][None])
                probs.append(prob.reshape(KB, TOK).astype(jnp.bfloat16))
                dscores.append(dscore.reshape(KB, TOK).astype(jnp.bfloat16))
            probs = jnp.concatenate(probs, axis=1)
            dscores = jnp.concatenate(dscores, axis=1)
            acc_v[keys_of(j), :] += dot(probs, os[...], nn)
            acc_k[keys_of(j), :] += dot(dscores, qs[...], nn)
            dq[...] += dot(kv[0, keys_of(j), :], dscores, tn)

        for h, span in heads():
            gq[row, :, span] = (dq[:, span].T * INV_ROOT).astype(jnp.bfloat16)

    dkv[0] = (acc_k[...] * INV_ROOT).astype(jnp.bfloat16)
    dkv[1] = acc_v[...].astype(jnp.bfloat16)


def attend(where, doc_lengths, qo, kv):
    rows = PER_KV * TOK
    vmem = pl.BlockSpec(memory_space=pltpu.VMEM)
    smem = pl.BlockSpec(memory_space=pltpu.SMEM)
    return pl.pallas_call(
        attend_kernel,
        out_shape=(
            jax.ShapeDtypeStruct((SIDE, TOK, GW), jnp.bfloat16),
            jax.ShapeDtypeStruct((2, WIN, HD), jnp.bfloat16),
        ),
        in_specs=[smem, smem, vmem, vmem],
        out_specs=(vmem, vmem),
        scratch_shapes=[
            pltpu.VMEM((rows, HD), jnp.bfloat16),
            pltpu.VMEM((rows, HD), jnp.bfloat16),
            pltpu.VMEM((STEPS, KB, rows), jnp.float32),
            pltpu.VMEM((STEPS, KB, rows), jnp.float32),
            pltpu.VMEM((HD, rows), jnp.float32),
            pltpu.VMEM((WIN, HD), jnp.float32),
            pltpu.VMEM((WIN, HD), jnp.float32),
            pltpu.VMEM((8, rows), jnp.float32),
            pltpu.VMEM((8, rows), jnp.float32),
            pltpu.VMEM((8, rows), jnp.float32),
        ],
        compiler_params=pltpu.CompilerParams(vmem_limit_bytes=34 * 1024 * 1024),
        name="attend",
    )(where, doc_lengths, qo, kv)


def emit_kernel(a, b, c, out_a, out_b, out_c, sems):
    copies = [
        pltpu.make_async_copy(src, dst, sems.at[i])
        for i, (src, dst) in enumerate(((a, out_a), (b, out_b), (c, out_c)))
    ]
    for copy in copies:
        copy.start()
    for copy in copies:
        copy.wait()


def emit(*results):
    return pl.pallas_call(
        emit_kernel,
        out_shape=tuple(jax.ShapeDtypeStruct(r.shape, r.dtype) for r in results),
        in_specs=[pl.BlockSpec(memory_space=pl.ANY)] * 3,
        out_specs=(pl.BlockSpec(memory_space=pltpu.HBM),) * 3,
        scratch_shapes=[pltpu.SemaphoreType.DMA((3,))],
        compiler_params=pltpu.CompilerParams(vmem_limit_bytes=1024 * 1024),
        name="emit",
    )(*results)


def local(queries, keys, values, grad_out, doc_lengths):
    qo, kv = gather(*(pltpu.with_memory_space_constraint(a, pltpu.HBM) for a in (queries, grad_out, keys, values)))
    where = jnp.stack([lax.axis_index("dp"), lax.rem(lax.axis_index("seq"), SIDE)]).astype(jnp.int32)
    gq, dkv = attend(where, doc_lengths, qo, kv.reshape(2, WIN, HD))
    return emit(*give_back(gq, dkv.reshape(2, 2, SIDE, SIDE, TOK, HD)))


def solution(mesh):
    split = P(("dp", "seq"), None)
    return jax.shard_map(
        local,
        mesh=mesh,
        in_specs=(split, split, split, split, P()),
        out_specs=(split, split, split),
        check_vma=False,
    )
```

```python
import functools

import jax
import jax.numpy as jnp
from jax import lax
from jax.experimental import pallas as pl
from jax.experimental.pallas import tpu as pltpu
from jax.sharding import PartitionSpec as P

MESH = pl.DeviceIdType.MESH
SIDE = 4
TOK = 128
HD = 128
GW = 1024
PER_KV = GW // HD
GROUP = SIDE * SIDE * TOK
WIN = 2 * GROUP
KB = 256
SLOTS = 24
EARLIEST = (0, 3, 8, 15)
FROM_X = (0, 1, 3, 2)
LOG2E = 1.4426950408889634
INV_ROOT = HD ** -0.5
LOW = -1e30
SCALE2 = INV_ROOT * LOG2E


def place():
    seq = lax.axis_index("seq")
    return lax.axis_index("dp"), lax.div(seq, SIDE), lax.rem(seq, SIDE)


def greet(dp, x, y):
    barrier = pltpu.get_barrier_semaphore()
    count = lax.axis_size("dp")
    peers = [{"seq": lax.rem(x + d, SIDE) * SIDE + y} for d in range(1, SIDE)]
    peers += [{"seq": x * SIDE + lax.rem(y + d, SIDE)} for d in range(1, SIDE)]
    peers += [{"dp": lax.rem(dp + 1, count)}, {"dp": lax.rem(dp + count - 1, count)}]
    for peer in peers:
        pl.semaphore_signal(barrier, inc=1, device_id=peer, device_id_type=MESH)
    pl.semaphore_wait(barrier, len(peers))


def cols(index, width):
    return pl.ds(pl.multiple_of(index * width, width), width)


def fold(tile):
    return tile.reshape(KB // 8, 8, HD)


def step_kernel(
    q, o, k, v, lens, out_q, out_k, out_v,
    land, kv, qs, os, s_buf, dp_buf, stats, run, final, dq, lows,
    gq, z_out, z_in, own, y_out, y_in, x_out, send, recv, here,
):
    dp, x, y = place()
    count = lax.axis_size("dp")
    used = [0]

    def remote(src, dst, device):
        i = used[0]
        used[0] += 1
        copy = pltpu.make_async_remote_copy(
            src_ref=src, dst_ref=dst, send_sem=send.at[i], recv_sem=recv.at[i],
            device_id=device, device_id_type=MESH,
        )
        copy.start()
        return copy

    def local_copy(src, dst, i):
        copy = pltpu.make_async_copy(src, dst, here.at[i])
        copy.start()
        return copy

    def at_x(d):
        return {"seq": lax.rem(x + d, SIDE) * SIDE + y}

    def at_y(d):
        return {"seq": x * SIDE + lax.rem(y + d, SIDE)}

    after = {"dp": lax.rem(dp + 1, count)}
    before = {"dp": lax.rem(dp + count - 1, count)}
    heads = [slice(h * HD, (h + 1) * HD) for h in range(PER_KV)]

    kv_here = [local_copy(a.at[:, cols(x, HD)], kv.at[n, 1, x, y], n) for n, a in enumerate((k, v))]
    q_here = [local_copy(a.at[:, cols(x, GW)], land.at[0, n], 2 + n) for n, a in enumerate((q, o))]
    greet(dp, x, y)
    first = []
    for d in (1, 3, 2):
        for n, a in enumerate((k, v)):
            head = lax.rem(x + d, SIDE)
            first.append(remote(a.at[:, cols(head, HD)], kv.at[n, 1, x, y], at_x(d)))
    arrive = {}
    for d in (3, 1, 2):
        slot = FROM_X.index(SIDE - d)
        head = lax.rem(x + d, SIDE)
        arrive[slot] = [
            remote(a.at[:, cols(head, GW)], land.at[slot, n], at_x(d)) for n, a in enumerate((q, o))
        ]

    def take(slot):
        for copy in q_here if slot == 0 else arrive[slot]:
            if slot == 0:
                copy.wait()
            else:
                copy.wait_recv()
        for h, span in enumerate(heads):
            qs[slot, span, :] = land[slot, 0, :, span]
            os[slot, span, :] = land[slot, 1, :, span]

    for copy in kv_here:
        copy.wait()
    for copy in first:
        copy.wait_recv()
    mine = kv.at[:, 1, :, y]
    along = [remote(mine, mine, at_y(d)) for d in (1, 3)]
    later = [remote(mine, kv.at[:, 0, :, y], after)]
    onward = []
    for copy, d in zip(along, (1, 3)):
        copy.wait_recv()
        source = lax.rem(y + SIDE - d, SIDE)
        part = kv.at[:, 1, pl.ds(d - 1 if d == 1 else 2, 2), source]
        onward.append(remote(part, part, at_y(d)))
        later.append(remote(kv.at[:, 1, :, source], kv.at[:, 0, :, source], after))
    take(0)
    run[...] = jnp.zeros_like(run)

    def at_least(value, bound):
        return (value >= bound).astype(jnp.int32)

    first_key = (dp - 1) * GROUP
    spots, steps, bases, blocks = [], [], [], []
    ready = jnp.int32(0)
    for slot in range(SIDE):
        block = lax.rem(x + FROM_X[slot], SIDE) * SIDE + y
        head_pos = dp * GROUP + block * TOK
        pos = head_pos + lax.broadcasted_iota(jnp.int32, (8, TOK), 1)

        def one_doc(i, state):
            end, low, low_row = state
            end = end + lens[i]
            low = jnp.maximum(low, end * at_least(head_pos, end))
            low_row = jnp.where(end <= pos, end, low_row)
            return end, low, low_row

        zero = jnp.int32(0)
        _, low, low_row = lax.fori_loop(
            0, lens.shape[0], one_doc, (zero, zero, jnp.zeros((8, TOK), jnp.int32))
        )
        lows[slot] = low_row - first_key
        end_block = GROUP // TOK + block + 1
        length = lax.div(end_block - lax.div(low - first_key, TOK) + 1, 2)
        spot = jnp.maximum(ready, EARLIEST[slot])
        ready = spot + length
        spots.append(spot)
        steps.append(length)
        bases.append(jnp.maximum(0, end_block - 2 * length))
        blocks.append(block)

    def pick(slot, values):
        picked = values[0]
        for n in range(1, SIDE):
            picked = picked + at_least(slot, n) * (values[n] - values[n - 1])
        return picked

    def step_of(i):
        slot = sum(at_least(i, spot) for spot in spots[1:])
        j = i - pick(slot, spots)
        lead = pick(slot, bases) + 2 * jnp.minimum(j, pick(slot, steps) - 1)
        return slot, j, jnp.minimum(lead, WIN // TOK - 2)

    def rows(n, lead):
        pieces = []
        for c in (lead, lead + 1):
            pieces.append(kv[n, lax.shift_right_logical(c, 4), lax.shift_right_logical(c, 2) & 3, c & 3])
        return jnp.concatenate(pieces, axis=0)

    nt = (((1,), (1,)), ((), ()))
    tn = (((0,), (0,)), ((), ()))
    nn = (((1,), (0,)), ((), ()))

    def dot(a, b, dims):
        return lax.dot_general(a, b, dims, preferred_element_type=jnp.float32)

    def score_step(i):
        slot, j, lead = step_of(i)
        scores = dot(rows(0, lead), qs[slot], nt)
        dprobs = dot(rows(1, lead), os[slot], nt)
        key = lead * TOK + lax.broadcasted_iota(jnp.int32, (KB, TOK), 0)
        last = GROUP + pick(slot, blocks) * TOK + lax.broadcasted_iota(jnp.int32, (KB, TOK), 1)
        new_block = jnp.broadcast_to(j, (8, HD)) == 0
        allowed = (key >= jnp.broadcast_to(lows[slot][0:1], (KB, TOK))) & (key <= last)
        for h, span in enumerate(heads):
            tile = jnp.where(allowed, scores[:, span] * SCALE2, LOW)
            s_buf[i, :, :, span] = tile.reshape(2, TOK, HD)
            dprob = dprobs[:, span]
            dp_buf[i, :, span] = dprob.astype(jnp.bfloat16)
            old = jnp.where(new_block, LOW, run[0, :, span])
            new = jnp.maximum(old, jnp.max(fold(tile), axis=0))
            weight = jnp.exp2(fold(tile) - new[None])
            shrink = jnp.exp2(old - new)
            norm = jnp.where(new_block, 0.0, run[1, :, span])
            dots = jnp.where(new_block, 0.0, run[2, :, span])
            norm = norm * shrink + jnp.sum(weight, axis=0)
            dots = dots * shrink + jnp.sum(weight * fold(dprob), axis=0)
            for n, value in enumerate((new, norm, dots)):
                run[n, :, span] = value
                stats[i, n, :, span] = value

    for copy, d in zip(onward, (1, 3)):
        copy.wait_recv()
    far = lax.rem(y + 2, SIDE)
    later.append(remote(kv.at[:, 1, :, far], kv.at[:, 0, :, far], after))
    for copy in later:
        copy.wait_recv()
    for slot in range(SIDE):
        if slot:
            take(slot)
        pl.loop(EARLIEST[slot], (EARLIEST + (SLOTS,))[slot + 1])(score_step)

    for slot in range(SIDE):
        end = jnp.minimum(spots[slot] + steps[slot], SLOTS) - 1
        part = stats[end, 0]
        peak = jnp.max(part, axis=0, keepdims=True)
        share = jnp.exp2(part - peak)
        total = jnp.sum(stats[end, 1] * share, axis=0, keepdims=True)
        delta = jnp.sum(stats[end, 2] * share, axis=0, keepdims=True) / total
        final[slot, 0] = jnp.broadcast_to(peak + jnp.log2(total), part.shape)
        final[slot, 1] = jnp.broadcast_to(delta, part.shape)

    dq[...] = jnp.zeros_like(dq)

    @pl.loop(0, SLOTS)
    def _(i):
        slot, j, lead = step_of(i)
        probs, dscores = [], []
        for h, span in enumerate(heads):
            prob = jnp.exp2(fold(s_buf[i, :, :, span]) - final[slot, 0, :, span][None])
            dprob = fold(dp_buf[i, :, span].astype(jnp.float32))
            dscore = prob * (dprob - final[slot, 1, :, span][None])
            probs.append(prob.reshape(KB, TOK).astype(jnp.bfloat16))
            dscores.append(dscore.reshape(KB, TOK).astype(jnp.bfloat16))
        probs = jnp.concatenate(probs, axis=1)
        dscores = jnp.concatenate(dscores, axis=1)
        s_buf[i, :, :, 0:HD] = dot(dscores, qs[slot], nn).reshape(2, TOK, HD)
        s_buf[i, :, :, HD:2 * HD] = dot(probs, os[slot], nn).reshape(2, TOK, HD)
        now = dq[...] * jnp.minimum(j, 1).astype(jnp.float32) + dot(rows(0, lead), dscores, tn)
        dq[...] = now
        dp_buf[i, 0:HD, :] = (now * INV_ROOT).astype(jnp.bfloat16)

    def key_sum(c):
        sums = [jnp.zeros((TOK, HD), jnp.float32)] * 2
        for slot in range(SIDE):
            off = c - bases[slot]
            inside = (at_least(off, 0) * at_least(2 * steps[slot] - 1, off)).astype(jnp.float32)
            i = jnp.clip(spots[slot] + lax.shift_right_arithmetic(off, 1), 0, SLOTS - 1)
            for n in range(2):
                sums[n] += inside * s_buf[i, off & 1, :, n * HD:(n + 1) * HD]
        return sums[0] * INV_ROOT, sums[1]

    down = {}
    order = (2, 1, 3, 0)
    for d in order:
        column = lax.rem(y + d, SIDE)

        @pl.loop(0, SIDE)
        def _(row):
            for n, total in enumerate(key_sum(row * SIDE + column)):
                z_out[d, n, row] = total.astype(jnp.bfloat16)

        down[d] = remote(z_out.at[d], z_in.at[d], before)

    back_q = []
    for slot in (3, 1, 2, 0):
        end = jnp.minimum(spots[slot] + steps[slot], SLOTS) - 1
        for h, span in enumerate(heads):
            gq[slot, :, span] = dp_buf[end, 0:HD, span].T
        if slot:
            back_q.append(remote(gq.at[slot], out_q.at[:, cols(x, GW)], at_x(FROM_X[slot])))
    own_q = local_copy(gq.at[0], out_q.at[:, cols(x, GW)], 4)

    across = {}
    for d in order:
        column = lax.rem(y + d, SIDE)

        @pl.loop(0, SIDE)
        def _(row):
            for n, total in enumerate(key_sum(GROUP // TOK + row * SIDE + column)):
                own[d, n, row] = total

    def total(d):
        down[d].wait_recv()
        return own[d] + z_in[d].astype(jnp.float32)

    for d in order[:3]:
        y_out[d - 1] = total(d).astype(jnp.bfloat16)
        across[d] = remote(y_out.at[d - 1], y_in.at[d - 1], at_y(d))
    rest = total(0)
    for d in order[:3]:
        across[d].wait_recv()
        rest = rest + y_in[d - 1].astype(jnp.float32)
    x_out[...] = rest.astype(jnp.bfloat16)
    back = []
    for d in (2, 1, 3):
        target = lax.rem(x + d, SIDE)
        for n, out in enumerate((out_k, out_v)):
            back.append(remote(x_out.at[n, target], out.at[:, cols(x, HD)], at_x(d)))
    own_kv = [local_copy(x_out.at[n, x], out.at[:, cols(x, HD)], 5 + n) for n, out in enumerate((out_k, out_v))]
    for copy in back_q + back:
        copy.wait_recv()
    for copy in [own_q] + own_kv:
        copy.wait()
    gone = first + along + later + onward + back_q + back
    for copies in list(arrive.values()) + [list(down.values()), list(across.values()), gone]:
        for copy in copies:
            copy.wait_send()


VMEM_GRANT = 57 * 1024 * 1024
COPIES = 6 + 6 + 2 + 2 + 4 + 4 + 3 + 3 + 6


def one_step(queries, grad_out, keys, values, doc_lengths):
    piece = (2, SIDE, TOK, HD)
    wide = PER_KV * TOK
    hbm = pl.BlockSpec(memory_space=pltpu.HBM)
    arguments = [
        pltpu.with_memory_space_constraint(a, pltpu.HBM) for a in (queries, grad_out, keys, values)
    ]
    return pl.pallas_call(
        step_kernel,
        out_shape=(
            jax.ShapeDtypeStruct((TOK, SIDE * GW), jnp.bfloat16),
            jax.ShapeDtypeStruct((TOK, SIDE * HD), jnp.bfloat16),
            jax.ShapeDtypeStruct((TOK, SIDE * HD), jnp.bfloat16),
        ),
        in_specs=[hbm] * 4 + [pl.BlockSpec(memory_space=pltpu.SMEM)],
        out_specs=(pl.BlockSpec(memory_space=pl.ANY),) * 3,
        scratch_shapes=[
            pltpu.VMEM((SIDE, 2, TOK, GW), jnp.bfloat16),
            pltpu.VMEM((2, 2, SIDE, SIDE, TOK, HD), jnp.bfloat16),
            pltpu.VMEM((SIDE, wide, HD), jnp.bfloat16),
            pltpu.VMEM((SIDE, wide, HD), jnp.bfloat16),
            pltpu.VMEM((SLOTS, 2, TOK, wide), jnp.float32),
            pltpu.VMEM((SLOTS, KB, wide), jnp.bfloat16),
            pltpu.VMEM((SLOTS, 3, 8, wide), jnp.float32),
            pltpu.VMEM((3, 8, wide), jnp.float32),
            pltpu.VMEM((SIDE, 2, 8, wide), jnp.float32),
            pltpu.VMEM((HD, wide), jnp.float32),
            pltpu.VMEM((SIDE, 8, TOK), jnp.int32),
            pltpu.VMEM((SIDE, TOK, GW), jnp.bfloat16),
            pltpu.VMEM((SIDE,) + piece, jnp.bfloat16),
            pltpu.VMEM((SIDE,) + piece, jnp.bfloat16),
            pltpu.VMEM((SIDE,) + piece, jnp.float32),
            pltpu.VMEM((3,) + piece, jnp.bfloat16),
            pltpu.VMEM((3,) + piece, jnp.bfloat16),
            pltpu.VMEM(piece, jnp.bfloat16),
            pltpu.SemaphoreType.DMA((COPIES,)),
            pltpu.SemaphoreType.DMA((COPIES,)),
            pltpu.SemaphoreType.DMA((7,)),
        ],
        compiler_params=pltpu.CompilerParams(
            collective_id=0, has_side_effects=True, vmem_limit_bytes=VMEM_GRANT
        ),
        name="step",
    )(*arguments, doc_lengths)


def emit_kernel(a, b, c, out_a, out_b, out_c, hold_a, hold_b, hold_c, into, out_of):
    pieces = []
    rows = TOK // 4
    for n in range(4):
        span = pl.ds(n * rows, rows)
        pieces.append((a.at[span], hold_a.at[span], out_a.at[span]))
    pieces += [(b, hold_b, out_b), (c, hold_c, out_c)]
    starts = [pltpu.make_async_copy(p[0], p[1], into.at[i]) for i, p in enumerate(pieces)]
    ends = [pltpu.make_async_copy(p[1], p[2], out_of.at[i]) for i, p in enumerate(pieces)]
    for copy in starts:
        copy.start()
    for start, end in zip(starts, ends):
        start.wait()
        end.start()
    for copy in ends:
        copy.wait()


def emit(*results):
    hbm = pl.BlockSpec(memory_space=pltpu.HBM)
    results = [pltpu.with_memory_space_constraint(r, pltpu.HBM) for r in results]
    return pl.pallas_call(
        emit_kernel,
        out_shape=tuple(jax.ShapeDtypeStruct(r.shape, r.dtype) for r in results),
        in_specs=[hbm] * 3,
        out_specs=(hbm,) * 3,
        scratch_shapes=[pltpu.VMEM(r.shape, r.dtype) for r in results]
        + [pltpu.SemaphoreType.DMA((6,)), pltpu.SemaphoreType.DMA((6,))],
        name="emit",
    )(*results)


def local(queries, keys, values, grad_out, doc_lengths):
    return emit(*one_step(queries, grad_out, keys, values, doc_lengths))


def solution(mesh):
    split = P(("dp", "seq"), None)
    return jax.shard_map(
        local,
        mesh=mesh,
        in_specs=(split, split, split, split, P()),
        out_specs=(split, split, split),
        check_vma=False,
    )
```

```python
import functools

import jax
import jax.numpy as jnp
from jax import lax
from jax.experimental import pallas as pl
from jax.experimental.pallas import tpu as pltpu
from jax.sharding import PartitionSpec as P

MESH = pl.DeviceIdType.MESH
SIDE = 4
TOK = 128
HD = 128
GW = 1024
PER_KV = GW // HD
GROUP = SIDE * SIDE * TOK
WIN = 2 * GROUP
KB = 256
SLOTS = 24
BEHIND = 15
EARLIEST = (0, 3, 8, 15)
FROM_X = (0, 1, 3, 2)
LOG2E = 1.4426950408889634
INV_ROOT = HD ** -0.5
LOW = -1e30
SCALE2 = INV_ROOT * LOG2E


def place():
    seq = lax.axis_index("seq")
    return lax.axis_index("dp"), lax.div(seq, SIDE), lax.rem(seq, SIDE)


def greet(dp, x, y):
    barrier = pltpu.get_barrier_semaphore()
    count = lax.axis_size("dp")
    peers = [{"seq": lax.rem(x + d, SIDE) * SIDE + y} for d in range(1, SIDE)]
    peers += [{"seq": x * SIDE + lax.rem(y + d, SIDE)} for d in range(1, SIDE)]
    peers += [{"dp": lax.rem(dp + 1, count)}, {"dp": lax.rem(dp + count - 1, count)}]
    for peer in peers:
        pl.semaphore_signal(barrier, inc=1, device_id=peer, device_id_type=MESH)
    pl.semaphore_wait(barrier, len(peers))


def cols(index, width):
    return pl.ds(pl.multiple_of(index * width, width), width)


def fold(tile):
    return tile.reshape(KB // 8, 8, HD)


def step_kernel(
    q, o, k, v, lens, out_q, out_k, out_v,
    land, kv, qs, os, s_buf, dp_buf, stats, run, final, dq, lows,
    terms, dqs, z_out, z_in, own, y_out, y_in, x_out, send, recv, here,
):
    dp, x, y = place()
    count = lax.axis_size("dp")
    used = [0]

    def remote(src, dst, device):
        i = used[0]
        used[0] += 1
        copy = pltpu.make_async_remote_copy(
            src_ref=src, dst_ref=dst, send_sem=send.at[i], recv_sem=recv.at[i],
            device_id=device, device_id_type=MESH,
        )
        copy.start()
        return copy

    def local_copy(src, dst, i):
        copy = pltpu.make_async_copy(src, dst, here.at[i])
        copy.start()
        return copy

    def at_x(d):
        return {"seq": lax.rem(x + d, SIDE) * SIDE + y}

    def at_y(d):
        return {"seq": x * SIDE + lax.rem(y + d, SIDE)}

    after = {"dp": lax.rem(dp + 1, count)}
    before = {"dp": lax.rem(dp + count - 1, count)}
    heads = [slice(h * HD, (h + 1) * HD) for h in range(PER_KV)]

    kv_here = [local_copy(a.at[:, cols(x, HD)], kv.at[n, 1, x, y], n) for n, a in enumerate((k, v))]
    q_here = [local_copy(a.at[:, cols(x, GW)], land.at[0, n], 2 + n) for n, a in enumerate((q, o))]
    greet(dp, x, y)
    first = []
    for d in (1, 3, 2):
        for n, a in enumerate((k, v)):
            head = lax.rem(x + d, SIDE)
            first.append(remote(a.at[:, cols(head, HD)], kv.at[n, 1, x, y], at_x(d)))
    arrive = {}
    for d in (3, 1, 2):
        slot = FROM_X.index(SIDE - d)
        head = lax.rem(x + d, SIDE)
        arrive[slot] = [
            remote(a.at[:, cols(head, GW)], land.at[slot, n], at_x(d)) for n, a in enumerate((q, o))
        ]

    def take(slot):
        for copy in q_here if slot == 0 else arrive[slot]:
            if slot == 0:
                copy.wait()
            else:
                copy.wait_recv()
        for h, span in enumerate(heads):
            qs[slot, span, :] = land[slot, 0, :, span]
            os[slot, span, :] = land[slot, 1, :, span]

    for copy in kv_here:
        copy.wait()
    for copy in first:
        copy.wait_recv()
    mine = kv.at[:, 1, :, y]
    along = [remote(mine, mine, at_y(d)) for d in (1, 3)]
    later = [remote(mine, kv.at[:, 0, :, y], after)]
    onward = []
    for copy, d in zip(along, (1, 3)):
        copy.wait_recv()
        source = lax.rem(y + SIDE - d, SIDE)
        part = kv.at[:, 1, pl.ds(d - 1 if d == 1 else 2, 2), source]
        onward.append(remote(part, part, at_y(d)))
        later.append(remote(kv.at[:, 1, :, source], kv.at[:, 0, :, source], after))
    take(0)
    run[...] = jnp.zeros_like(run)

    def at_least(value, bound):
        return (value >= bound).astype(jnp.int32)

    first_key = (dp - 1) * GROUP
    spots, steps, bases, blocks = [], [], [], []
    ready = jnp.int32(0)
    for slot in range(SIDE):
        block = lax.rem(x + FROM_X[slot], SIDE) * SIDE + y
        head_pos = dp * GROUP + block * TOK
        pos = head_pos + lax.broadcasted_iota(jnp.int32, (8, TOK), 1)

        def one_doc(i, state):
            end, low, low_row = state
            end = end + lens[i]
            low = jnp.maximum(low, end * at_least(head_pos, end))
            low_row = jnp.where(end <= pos, end, low_row)
            return end, low, low_row

        zero = jnp.int32(0)
        _, low, low_row = lax.fori_loop(
            0, lens.shape[0], one_doc, (zero, zero, jnp.zeros((8, TOK), jnp.int32))
        )
        lows[slot] = low_row - first_key
        end_block = GROUP // TOK + block + 1
        length = lax.div(end_block - lax.div(low - first_key, TOK) + 1, 2)
        spot = jnp.maximum(ready, EARLIEST[slot])
        ready = spot + length
        spots.append(spot)
        steps.append(length)
        bases.append(jnp.maximum(0, end_block - 2 * length))
        blocks.append(block)

    def pick(slot, values):
        picked = values[0]
        for n in range(1, SIDE):
            picked = picked + at_least(slot, n) * (values[n] - values[n - 1])
        return picked

    def step_of(i):
        slot = sum(at_least(i, spot) for spot in spots[1:])
        j = i - pick(slot, spots)
        lead = pick(slot, bases) + 2 * jnp.minimum(j, pick(slot, steps) - 1)
        return slot, j, jnp.minimum(lead, WIN // TOK - 2)

    def rows(n, lead):
        pieces = []
        for c in (lead, lead + 1):
            pieces.append(kv[n, lax.shift_right_logical(c, 4), lax.shift_right_logical(c, 2) & 3, c & 3])
        return jnp.concatenate(pieces, axis=0)

    nt = (((1,), (1,)), ((), ()))
    tn = (((0,), (0,)), ((), ()))
    nn = (((1,), (0,)), ((), ()))

    def dot(a, b, dims):
        return lax.dot_general(a, b, dims, preferred_element_type=jnp.float32)

    def score_step(i):
        slot, j, lead = step_of(i)
        scores = dot(rows(0, lead), qs[slot], nt)
        dprobs = dot(rows(1, lead), os[slot], nt)
        key = lead * TOK + lax.broadcasted_iota(jnp.int32, (KB, TOK), 0)
        last = GROUP + pick(slot, blocks) * TOK + lax.broadcasted_iota(jnp.int32, (KB, TOK), 1)
        new_block = jnp.broadcast_to(j, (8, HD)) == 0
        allowed = (key >= jnp.broadcast_to(lows[slot][0:1], (KB, TOK))) & (key <= last)
        for h, span in enumerate(heads):
            tile = jnp.where(allowed, scores[:, span] * SCALE2, LOW)
            s_buf[i, :, :, span] = tile.reshape(2, TOK, HD)
            dprob = dprobs[:, span]
            dprob = dprob.astype(jnp.bfloat16)
            dp_buf[i, :, span] = dprob
            dprob = dprob.astype(jnp.float32)
            old = jnp.where(new_block, LOW, run[0, :, span])
            new = jnp.maximum(old, jnp.max(fold(tile), axis=0))
            weight = jnp.exp2(fold(tile) - new[None])
            shrink = jnp.exp2(old - new)
            norm = jnp.where(new_block, 0.0, run[1, :, span])
            dots = jnp.where(new_block, 0.0, run[2, :, span])
            norm = norm * shrink + jnp.sum(weight, axis=0)
            dots = dots * shrink + jnp.sum(weight * fold(dprob), axis=0)
            for n, value in enumerate((new, norm, dots)):
                run[n, :, span] = value
                stats[i, n, :, span] = value

    for copy, d in zip(onward, (1, 3)):
        copy.wait_recv()
    far = lax.rem(y + 2, SIDE)
    later.append(remote(kv.at[:, 1, :, far], kv.at[:, 0, :, far], after))
    for copy in later:
        copy.wait_recv()
    for slot in range(SIDE):
        if slot:
            take(slot)
        pl.loop(EARLIEST[slot], (EARLIEST + (SLOTS,))[slot + 1])(score_step)

    for slot in range(SIDE):
        end = jnp.minimum(spots[slot] + steps[slot], SLOTS) - 1
        part = stats[end, 0]
        peak = jnp.max(part, axis=0, keepdims=True)
        share = jnp.exp2(part - peak)
        total = jnp.sum(stats[end, 1] * share, axis=0, keepdims=True)
        delta = jnp.sum(stats[end, 2] * share, axis=0, keepdims=True) / total
        final[slot, 0] = jnp.broadcast_to(peak + jnp.log2(total), part.shape)
        final[slot, 1] = jnp.broadcast_to(delta, part.shape)

    behind = [
        jnp.clip(lax.shift_right_arithmetic(17 - bases[slot], 1), 0, steps[slot])
        for slot in range(SIDE)
    ]
    counts = behind + [steps[slot] - behind[slot] for slot in range(SIDE)]
    opens = [jnp.int32(0)]
    for n in range(2 * SIDE - 1):
        opens.append(opens[-1] + counts[n])

    def pick_run(run, values):
        picked = values[0]
        for n in range(1, 2 * SIDE):
            picked = picked + at_least(run, n) * (values[n] - values[n - 1])
        return picked

    dq[...] = jnp.zeros_like(dq)

    def grad_step(t):
        part = sum(at_least(t, begin) for begin in opens[1:])
        slot = part & 3
        j = t - pick_run(part, opens)
        at = jnp.minimum(j + at_least(part, SIDE) * pick(slot, behind), pick(slot, steps) - 1)
        lead = jnp.minimum(pick(slot, bases) + 2 * at, WIN // TOK - 2)
        i = jnp.clip(pick(slot, spots) + at, 0, SLOTS - 1)
        probs, dscores = [], []
        for h, span in enumerate(heads):
            prob = jnp.exp2(fold(s_buf[i, :, :, span]) - final[slot, 0, :, span][None])
            dprob = fold(dp_buf[i, :, span].astype(jnp.float32))
            dscore = prob * (dprob - final[slot, 1, :, span][None])
            probs.append(prob.reshape(KB, TOK).astype(jnp.bfloat16))
            dscores.append(dscore.reshape(KB, TOK).astype(jnp.bfloat16))
        probs = jnp.concatenate(probs, axis=1)
        dscores = jnp.concatenate(dscores, axis=1)
        terms[t, 1] = dot(probs, os[slot], nn).reshape(2, TOK, HD)
        terms[t, 0] = dot(dscores, qs[slot], nn).reshape(2, TOK, HD)
        now = dq[...] * jnp.clip(j, 0, 1).astype(jnp.float32) + dot(rows(0, lead), dscores, tn)
        dq[...] = now
        dqs[t] = (now * INV_ROOT).astype(jnp.bfloat16)

    def key_sum(c):
        sums = [jnp.zeros((TOK, HD), jnp.float32)] * 2
        for slot in range(SIDE):
            off = c - bases[slot]
            inside = (at_least(off, 0) * at_least(2 * steps[slot] - 1, off)).astype(jnp.float32)
            j = lax.shift_right_arithmetic(off, 1)
            own_part = at_least(j, behind[slot])
            t = j + opens[slot] + own_part * (opens[SIDE + slot] - opens[slot] - behind[slot])
            t = jnp.clip(t, 0, SLOTS - 1)
            for n in range(2):
                sums[n] += inside * terms[t, n, off & 1]
        return sums[0] * INV_ROOT, sums[1]

    order = (2, 1, 3, 0)
    pl.loop(0, BEHIND)(grad_step)
    down = {}
    for d in order:
        row = lax.rem(x + d, SIDE)

        @pl.loop(0, SIDE)
        def _(column):
            for n, total in enumerate(key_sum(row * SIDE + column)):
                z_out[d, n, column] = total.astype(jnp.bfloat16)

        down[d] = remote(z_out.at[d], z_in.at[d], before)
    pl.loop(BEHIND, SLOTS)(grad_step)

    back_q = []
    for slot in (3, 1, 2, 0):
        ends = []
        for n in (slot, SIDE + slot):
            held = jnp.clip(opens[n] + counts[n] - 1, 0, SLOTS - 1)
            ends.append((held, at_least(counts[n], 1).astype(jnp.float32)))
        for h, span in enumerate(heads):
            block = sum(weight * dqs[held, :, span].astype(jnp.float32) for held, weight in ends)
            land[slot, 0, :, span] = block.T.astype(jnp.bfloat16)
        if slot:
            back_q.append(remote(land.at[slot, 0], out_q.at[:, cols(x, GW)], at_x(FROM_X[slot])))
    own_q = local_copy(land.at[0, 0], out_q.at[:, cols(x, GW)], 4)

    across, back = {}, []

    def finish(d):
        rest = own[order.index(d) % 2, :, y]
        for e in (1, 2, 3):
            across[d][e].wait_recv()
            rest = rest + y_in[d, e - 1].astype(jnp.float32)
        x_out[d] = rest.astype(jnp.bfloat16)
        if d:
            for n, out in enumerate((out_k, out_v)):
                back.append(remote(x_out.at[d, n], out.at[:, cols(x, HD)], at_x(d)))

    for n, d in enumerate(order):
        row, side = lax.rem(x + d, SIDE), n % 2

        @pl.loop(0, SIDE)
        def _(column):
            for n, total in enumerate(key_sum(GROUP // TOK + row * SIDE + column)):
                own[side, n, column] = total

        down[d].wait_recv()
        own[side] = own[side] + z_in[d].astype(jnp.float32)
        across[d] = {}
        for e in (2, 1, 3):
            y_out[d, e - 1] = own[side, :, lax.rem(y + e, SIDE)].astype(jnp.bfloat16)
            across[d][e] = remote(y_out.at[d, e - 1], y_in.at[d, e - 1], at_y(e))
        if n:
            finish(order[n - 1])
    finish(order[-1])
    own_kv = [local_copy(x_out.at[0, n], out.at[:, cols(x, HD)], 5 + n) for n, out in enumerate((out_k, out_v))]
    for copy in back_q + back:
        copy.wait_recv()
    for copy in [own_q] + own_kv:
        copy.wait()
    gone = first + along + later + onward + back_q + back
    gone += [copy for copies in across.values() for copy in copies.values()]
    for copies in list(arrive.values()) + [list(down.values()), gone]:
        for copy in copies:
            copy.wait_send()


VMEM_GRANT = 67043328
COPIES = 6 + 6 + 2 + 2 + 4 + 4 + 3 + 12 + 6


def one_step(queries, grad_out, keys, values, doc_lengths):
    piece = (2, SIDE, TOK, HD)
    wide = PER_KV * TOK
    hbm = pl.BlockSpec(memory_space=pltpu.HBM)
    arguments = [
        pltpu.with_memory_space_constraint(a, pltpu.HBM) for a in (queries, grad_out, keys, values)
    ]
    return pl.pallas_call(
        step_kernel,
        out_shape=(
            jax.ShapeDtypeStruct((TOK, SIDE * GW), jnp.bfloat16),
            jax.ShapeDtypeStruct((TOK, SIDE * HD), jnp.bfloat16),
            jax.ShapeDtypeStruct((TOK, SIDE * HD), jnp.bfloat16),
        ),
        in_specs=[hbm] * 4 + [pl.BlockSpec(memory_space=pltpu.SMEM)],
        out_specs=(pl.BlockSpec(memory_space=pl.ANY),) * 3,
        scratch_shapes=[
            pltpu.VMEM((SIDE, 2, TOK, GW), jnp.bfloat16),
            pltpu.VMEM((2, 2, SIDE, SIDE, TOK, HD), jnp.bfloat16),
            pltpu.VMEM((SIDE, wide, HD), jnp.bfloat16),
            pltpu.VMEM((SIDE, wide, HD), jnp.bfloat16),
            pltpu.VMEM((SLOTS, 2, TOK, wide), jnp.float32),
            pltpu.VMEM((SLOTS, KB, wide), jnp.bfloat16),
            pltpu.VMEM((SLOTS, 3, 8, wide), jnp.float32),
            pltpu.VMEM((3, 8, wide), jnp.float32),
            pltpu.VMEM((SIDE, 2, 8, wide), jnp.float32),
            pltpu.VMEM((HD, wide), jnp.float32),
            pltpu.VMEM((SIDE, 8, TOK), jnp.int32),
            pltpu.VMEM((SLOTS, 2, 2, TOK, HD), jnp.float32),
            pltpu.VMEM((SLOTS, HD, wide), jnp.bfloat16),
            pltpu.VMEM((SIDE,) + piece, jnp.bfloat16),
            pltpu.VMEM((SIDE,) + piece, jnp.bfloat16),
            pltpu.VMEM((2,) + piece, jnp.float32),
            pltpu.VMEM((SIDE, 3, 2, TOK, HD), jnp.bfloat16),
            pltpu.VMEM((SIDE, 3, 2, TOK, HD), jnp.bfloat16),
            pltpu.VMEM((SIDE, 2, TOK, HD), jnp.bfloat16),
            pltpu.SemaphoreType.DMA((COPIES,)),
            pltpu.SemaphoreType.DMA((COPIES,)),
            pltpu.SemaphoreType.DMA((7,)),
        ],
        compiler_params=pltpu.CompilerParams(
            collective_id=0, has_side_effects=True, vmem_limit_bytes=VMEM_GRANT
        ),
        name="step",
    )(*arguments, doc_lengths)


def emit_kernel(a, b, c, out_a, out_b, out_c, hold_a, hold_b, hold_c, into, out_of):
    pieces = []
    rows = TOK // 4
    for n in range(4):
        span = pl.ds(n * rows, rows)
        pieces.append((a.at[span], hold_a.at[span], out_a.at[span]))
    pieces += [(b, hold_b, out_b), (c, hold_c, out_c)]
    starts = [pltpu.make_async_copy(p[0], p[1], into.at[i]) for i, p in enumerate(pieces)]
    ends = [pltpu.make_async_copy(p[1], p[2], out_of.at[i]) for i, p in enumerate(pieces)]
    for copy in starts:
        copy.start()
    for start, end in zip(starts, ends):
        start.wait()
        end.start()
    for copy in ends:
        copy.wait()


def emit(*results):
    hbm = pl.BlockSpec(memory_space=pltpu.HBM)
    results = [pltpu.with_memory_space_constraint(r, pltpu.HBM) for r in results]
    return pl.pallas_call(
        emit_kernel,
        out_shape=tuple(jax.ShapeDtypeStruct(r.shape, r.dtype) for r in results),
        in_specs=[hbm] * 3,
        out_specs=(hbm,) * 3,
        scratch_shapes=[pltpu.VMEM(r.shape, r.dtype) for r in results]
        + [pltpu.SemaphoreType.DMA((6,)), pltpu.SemaphoreType.DMA((6,))],
        name="emit",
    )(*results)


def local(queries, keys, values, grad_out, doc_lengths):
    return emit(*one_step(queries, grad_out, keys, values, doc_lengths))


def solution(mesh):
    split = P(("dp", "seq"), None)
    return jax.shard_map(
        local,
        mesh=mesh,
        in_specs=(split, split, split, split, P()),
        out_specs=(split, split, split),
        check_vma=False,
    )
```

```python
import functools

import jax
import jax.numpy as jnp
from jax import lax
from jax.experimental import pallas as pl
from jax.experimental.pallas import tpu as pltpu
from jax.sharding import PartitionSpec as P

MESH = pl.DeviceIdType.MESH
SIDE = 4
TOK = 128
HD = 128
GW = 1024
PER_KV = GW // HD
GROUP = SIDE * SIDE * TOK
WIN = 2 * GROUP
KB = 256
SLOTS = 24
BEHIND = 15
EARLIEST = (0, 3, 8, 15)
FROM_X = (0, 1, 3, 2)
LOG2E = 1.4426950408889634
INV_ROOT = HD ** -0.5
LOW = -1e30
SCALE2 = INV_ROOT * LOG2E


def place():
    seq = lax.axis_index("seq")
    return lax.axis_index("dp"), lax.div(seq, SIDE), lax.rem(seq, SIDE)


def greet(dp, x, y):
    barrier = pltpu.get_barrier_semaphore()
    count = lax.axis_size("dp")
    peers = [{"seq": lax.rem(x + d, SIDE) * SIDE + y} for d in range(1, SIDE)]
    peers += [{"seq": x * SIDE + lax.rem(y + d, SIDE)} for d in range(1, SIDE)]
    peers += [{"dp": lax.rem(dp + 1, count)}, {"dp": lax.rem(dp + count - 1, count)}]
    for peer in peers:
        pl.semaphore_signal(barrier, inc=1, device_id=peer, device_id_type=MESH)
    pl.semaphore_wait(barrier, len(peers))


def cols(index, width):
    return pl.ds(pl.multiple_of(index * width, width), width)


def fold(tile):
    return tile.reshape(KB // 8, 8, HD)


def step_kernel(
    q, o, k, v, lens, out_q, out_k, out_v,
    land, kv, qs, os, s_buf, dp_buf, stats, run, final, dq, lows,
    terms, dqs, z_in, own, y_in, x_out, send, recv, here,
):
    dp, x, y = place()
    count = lax.axis_size("dp")
    used = [0]

    def remote(src, dst, device):
        i = used[0]
        used[0] += 1
        copy = pltpu.make_async_remote_copy(
            src_ref=src, dst_ref=dst, send_sem=send.at[i], recv_sem=recv.at[i],
            device_id=device, device_id_type=MESH,
        )
        copy.start()
        return copy

    def local_copy(src, dst, i):
        copy = pltpu.make_async_copy(src, dst, here.at[i])
        copy.start()
        return copy

    def at_x(d):
        return {"seq": lax.rem(x + d, SIDE) * SIDE + y}

    def at_y(d):
        return {"seq": x * SIDE + lax.rem(y + d, SIDE)}

    after = {"dp": lax.rem(dp + 1, count)}
    before = {"dp": lax.rem(dp + count - 1, count)}
    heads = [slice(h * HD, (h + 1) * HD) for h in range(PER_KV)]

    kv_here = [local_copy(a.at[:, cols(x, HD)], kv.at[n, 1, x, y], n) for n, a in enumerate((k, v))]
    q_here = [local_copy(a.at[:, cols(x, GW)], land.at[0, n], 2 + n) for n, a in enumerate((q, o))]
    greet(dp, x, y)
    first = []
    for d in (1, 3, 2):
        for n, a in enumerate((k, v)):
            head = lax.rem(x + d, SIDE)
            first.append(remote(a.at[:, cols(head, HD)], kv.at[n, 1, x, y], at_x(d)))
    arrive = {}
    for d in (3, 1, 2):
        slot = FROM_X.index(SIDE - d)
        head = lax.rem(x + d, SIDE)
        arrive[slot] = [
            remote(a.at[:, cols(head, GW)], land.at[slot, n], at_x(d)) for n, a in enumerate((q, o))
        ]

    def take(slot):
        for copy in q_here if slot == 0 else arrive[slot]:
            if slot == 0:
                copy.wait()
            else:
                copy.wait_recv()
        for h, span in enumerate(heads):
            qs[slot, span, :] = land[slot, 0, :, span]
            os[slot, span, :] = land[slot, 1, :, span]

    for copy in kv_here:
        copy.wait()
    for copy in first:
        copy.wait_recv()
    mine = kv.at[:, 1, :, y]
    along = [remote(mine, mine, at_y(d)) for d in (1, 3)]
    later = [remote(mine, kv.at[:, 0, :, y], after)]
    onward = []
    for copy, d in zip(along, (1, 3)):
        copy.wait_recv()
        source = lax.rem(y + SIDE - d, SIDE)
        part = kv.at[:, 1, pl.ds(d - 1 if d == 1 else 2, 2), source]
        onward.append(remote(part, part, at_y(d)))
        later.append(remote(kv.at[:, 1, :, source], kv.at[:, 0, :, source], after))
    take(0)
    run[...] = jnp.zeros_like(run)

    def at_least(value, bound):
        return (value >= bound).astype(jnp.int32)

    first_key = (dp - 1) * GROUP
    spots, steps, bases, blocks = [], [], [], []
    ready = jnp.int32(0)
    for slot in range(SIDE):
        block = lax.rem(x + FROM_X[slot], SIDE) * SIDE + y
        head_pos = dp * GROUP + block * TOK
        pos = head_pos + lax.broadcasted_iota(jnp.int32, (8, TOK), 1)

        def one_doc(i, state):
            end, low, low_row = state
            end = end + lens[i]
            low = jnp.maximum(low, end * at_least(head_pos, end))
            low_row = jnp.where(end <= pos, end, low_row)
            return end, low, low_row

        zero = jnp.int32(0)
        _, low, low_row = lax.fori_loop(
            0, lens.shape[0], one_doc, (zero, zero, jnp.zeros((8, TOK), jnp.int32))
        )
        lows[slot] = low_row - first_key
        end_block = GROUP // TOK + block + 1
        length = lax.div(end_block - lax.div(low - first_key, TOK) + 1, 2)
        spot = jnp.maximum(ready, EARLIEST[slot])
        ready = spot + length
        spots.append(spot)
        steps.append(length)
        bases.append(jnp.maximum(0, end_block - 2 * length))
        blocks.append(block)

    def pick(slot, values):
        picked = values[0]
        for n in range(1, SIDE):
            picked = picked + at_least(slot, n) * (values[n] - values[n - 1])
        return picked

    def step_of(i):
        slot = sum(at_least(i, spot) for spot in spots[1:])
        j = i - pick(slot, spots)
        lead = pick(slot, bases) + 2 * jnp.minimum(j, pick(slot, steps) - 1)
        return slot, j, jnp.minimum(lead, WIN // TOK - 2)

    def rows(n, lead):
        pieces = []
        for c in (lead, lead + 1):
            pieces.append(kv[n, lax.shift_right_logical(c, 4), lax.shift_right_logical(c, 2) & 3, c & 3])
        return jnp.concatenate(pieces, axis=0)

    nt = (((1,), (1,)), ((), ()))
    tn = (((0,), (0,)), ((), ()))
    nn = (((1,), (0,)), ((), ()))

    def dot(a, b, dims):
        return lax.dot_general(a, b, dims, preferred_element_type=jnp.float32)

    def score_step(i):
        slot, j, lead = step_of(i)
        scores = dot(rows(0, lead), qs[slot], nt)
        dprobs = dot(rows(1, lead), os[slot], nt)
        key = lead * TOK + lax.broadcasted_iota(jnp.int32, (KB, TOK), 0)
        last = GROUP + pick(slot, blocks) * TOK + lax.broadcasted_iota(jnp.int32, (KB, TOK), 1)
        new_block = jnp.broadcast_to(j, (8, HD)) == 0
        allowed = (key >= jnp.broadcast_to(lows[slot][0:1], (KB, TOK))) & (key <= last)
        for h, span in enumerate(heads):
            tile = jnp.where(allowed, scores[:, span] * SCALE2, LOW)
            s_buf[i, :, :, span] = tile.reshape(2, TOK, HD)
            dprob = dprobs[:, span]
            dprob = dprob.astype(jnp.bfloat16)
            dp_buf[i, :, span] = dprob
            dprob = dprob.astype(jnp.float32)
            old = jnp.where(new_block, LOW, run[0, :, span])
            new = jnp.maximum(old, jnp.max(fold(tile), axis=0))
            weight = jnp.exp2(fold(tile) - new[None])
            shrink = jnp.exp2(old - new)
            norm = jnp.where(new_block, 0.0, run[1, :, span])
            dots = jnp.where(new_block, 0.0, run[2, :, span])
            norm = norm * shrink + jnp.sum(weight, axis=0)
            dots = dots * shrink + jnp.sum(weight * fold(dprob), axis=0)
            for n, value in enumerate((new, norm, dots)):
                run[n, :, span] = value
                stats[i, n, :, span] = value

    for copy, d in zip(onward, (1, 3)):
        copy.wait_recv()
    far = lax.rem(y + 2, SIDE)
    later.append(remote(kv.at[:, 1, :, far], kv.at[:, 0, :, far], after))
    for copy in later:
        copy.wait_recv()
    for slot in range(SIDE):
        if slot:
            take(slot)
        pl.loop(EARLIEST[slot], (EARLIEST + (SLOTS,))[slot + 1])(score_step)

    for slot in range(SIDE):
        end = jnp.minimum(spots[slot] + steps[slot], SLOTS) - 1
        part = stats[end, 0]
        peak = jnp.max(part, axis=0, keepdims=True)
        share = jnp.exp2(part - peak)
        total = jnp.sum(stats[end, 1] * share, axis=0, keepdims=True)
        delta = jnp.sum(stats[end, 2] * share, axis=0, keepdims=True) / total
        final[slot, 0] = jnp.broadcast_to(peak + jnp.log2(total), part.shape)
        final[slot, 1] = jnp.broadcast_to(delta, part.shape)

    behind = [
        jnp.clip(lax.shift_right_arithmetic(17 - bases[slot], 1), 0, steps[slot])
        for slot in range(SIDE)
    ]
    counts = behind + [steps[slot] - behind[slot] for slot in range(SIDE)]
    opens = [jnp.int32(0)]
    for n in range(2 * SIDE - 1):
        opens.append(opens[-1] + counts[n])

    def pick_run(run, values):
        picked = values[0]
        for n in range(1, 2 * SIDE):
            picked = picked + at_least(run, n) * (values[n] - values[n - 1])
        return picked

    dq[...] = jnp.zeros_like(dq)

    def grad_step(t):
        part = sum(at_least(t, begin) for begin in opens[1:])
        slot = part & 3
        j = t - pick_run(part, opens)
        at = jnp.minimum(j + at_least(part, SIDE) * pick(slot, behind), pick(slot, steps) - 1)
        lead = jnp.minimum(pick(slot, bases) + 2 * at, WIN // TOK - 2)
        i = jnp.clip(pick(slot, spots) + at, 0, SLOTS - 1)
        probs, dscores = [], []
        for h, span in enumerate(heads):
            prob = jnp.exp2(fold(s_buf[i, :, :, span]) - final[slot, 0, :, span][None])
            dprob = fold(dp_buf[i, :, span].astype(jnp.float32))
            dscore = prob * (dprob - final[slot, 1, :, span][None])
            probs.append(prob.reshape(KB, TOK).astype(jnp.bfloat16))
            dscores.append(dscore.reshape(KB, TOK).astype(jnp.bfloat16))
        probs = jnp.concatenate(probs, axis=1)
        dscores = jnp.concatenate(dscores, axis=1)
        terms[t, 1] = dot(probs, os[slot], nn).reshape(2, TOK, HD)
        terms[t, 0] = dot(dscores, qs[slot], nn).reshape(2, TOK, HD)
        now = dq[...] * jnp.clip(j, 0, 1).astype(jnp.float32) + dot(rows(0, lead), dscores, tn)
        dq[...] = now
        dqs[t] = now.astype(jnp.bfloat16)

    def key_sum(c):
        sums = [jnp.zeros((TOK, HD), jnp.float32)] * 2
        for slot in range(SIDE):
            off = c - bases[slot]
            inside = (at_least(off, 0) * at_least(2 * steps[slot] - 1, off)).astype(jnp.float32)
            j = lax.shift_right_arithmetic(off, 1)
            own_part = at_least(j, behind[slot])
            t = j + opens[slot] + own_part * (opens[SIDE + slot] - opens[slot] - behind[slot])
            t = jnp.clip(t, 0, SLOTS - 1)
            for n in range(2):
                sums[n] += inside * terms[t, n, off & 1]
        return sums[0] * INV_ROOT, sums[1]

    order = (2, 1, 3, 0)
    pl.loop(0, BEHIND)(grad_step)
    down = {}
    for d in order:
        row = lax.rem(x + d, SIDE)

        @pl.loop(0, SIDE)
        def _(column):
            for n, total in enumerate(key_sum(row * SIDE + column)):
                kv[n, 0, row, column] = total.astype(jnp.bfloat16)

        if d:
            down[d] = [remote(kv.at[:, 0, row], z_in.at[d], before)]
        else:
            down[d] = []
            for e in order:
                column = lax.rem(y + e, SIDE)
                down[d].append(remote(kv.at[:, 0, row, column], z_in.at[d, :, column], before))
    pl.loop(BEHIND, SLOTS)(grad_step)

    back_q = []
    for slot in (3, 1, 2, 0):
        ends = []
        for n in (slot, SIDE + slot):
            held = jnp.clip(opens[n] + counts[n] - 1, 0, SLOTS - 1)
            ends.append((held, at_least(counts[n], 1).astype(jnp.float32) * INV_ROOT))
        for h, span in enumerate(heads):
            block = sum(weight * dqs[held, :, span].astype(jnp.float32) for held, weight in ends)
            land[slot, 0, :, span] = block.T.astype(jnp.bfloat16)
        if slot:
            back_q.append(remote(land.at[slot, 0], out_q.at[:, cols(x, GW)], at_x(FROM_X[slot])))
    own_q = local_copy(land.at[0, 0], out_q.at[:, cols(x, GW)], 4)

    across, back = {}, []

    def finish(d):
        for e in (1, 2, 3):
            across[d][e].wait_recv()
        for n in range(2):
            rest = own[order.index(d) % 2, n, y]
            for e in (1, 2, 3):
                rest = rest + y_in[d, e - 1, :, n * HD:(n + 1) * HD].astype(jnp.float32)
            x_out[d, n] = rest.astype(jnp.bfloat16)
        if d:
            for n, out in enumerate((out_k, out_v)):
                back.append(remote(x_out.at[d, n], out.at[:, cols(x, HD)], at_x(d)))

    for n, d in enumerate(order):
        row, side = lax.rem(x + d, SIDE), n % 2

        @pl.loop(0, SIDE)
        def _(column):
            for n, total in enumerate(key_sum(GROUP // TOK + row * SIDE + column)):
                own[side, n, column] = total

        across[d] = {}
        for e in order:
            if d == 0 or e == order[0]:
                down[d][order.index(e) if d == 0 else 0].wait_recv()
            column = lax.rem(y + e, SIDE)
            whole = own[side, :, column] + z_in[d, :, column].astype(jnp.float32)
            if e:
                leave = slice((e - 1) * 2 * HD, e * 2 * HD)
                land[d, 1, :, leave] = jnp.concatenate([whole[0], whole[1]], axis=1).astype(jnp.bfloat16)
                across[d][e] = remote(land.at[d, 1, :, leave], y_in.at[d, e - 1], at_y(e))
            else:
                own[side, :, column] = whole
        if n:
            finish(order[n - 1])
    finish(order[-1])
    own_kv = [local_copy(x_out.at[0, n], out.at[:, cols(x, HD)], 5 + n) for n, out in enumerate((out_k, out_v))]
    for copy in back_q + back:
        copy.wait_recv()
    for copy in [own_q] + own_kv:
        copy.wait()
    gone = first + along + later + onward + back_q + back
    gone += [copy for copies in across.values() for copy in copies.values()]
    for copies in list(arrive.values()) + list(down.values()) + [gone]:
        for copy in copies:
            copy.wait_send()


VMEM_GRANT = 65536000
COPIES = 6 + 6 + 2 + 2 + 4 + 7 + 3 + 12 + 6


def one_step(queries, grad_out, keys, values, doc_lengths):
    piece = (2, SIDE, TOK, HD)
    wide = PER_KV * TOK
    hbm = pl.BlockSpec(memory_space=pltpu.HBM)
    arguments = [
        pltpu.with_memory_space_constraint(a, pltpu.HBM) for a in (queries, grad_out, keys, values)
    ]
    return pl.pallas_call(
        step_kernel,
        out_shape=(
            pltpu.VMEM((TOK, SIDE * GW), jnp.bfloat16),
            pltpu.VMEM((TOK, SIDE * HD), jnp.bfloat16),
            pltpu.VMEM((TOK, SIDE * HD), jnp.bfloat16),
        ),
        in_specs=[hbm] * 4 + [pl.BlockSpec(memory_space=pltpu.SMEM)],
        out_specs=(pl.BlockSpec(memory_space=pl.ANY),) * 3,
        scratch_shapes=[
            pltpu.VMEM((SIDE, 2, TOK, GW), jnp.bfloat16),
            pltpu.VMEM((2, 2, SIDE, SIDE, TOK, HD), jnp.bfloat16),
            pltpu.VMEM((SIDE, wide, HD), jnp.bfloat16),
            pltpu.VMEM((SIDE, wide, HD), jnp.bfloat16),
            pltpu.VMEM((SLOTS, 2, TOK, wide), jnp.float32),
            pltpu.VMEM((SLOTS, KB, wide), jnp.bfloat16),
            pltpu.VMEM((SLOTS, 3, 8, wide), jnp.float32),
            pltpu.VMEM((3, 8, wide), jnp.float32),
            pltpu.VMEM((SIDE, 2, 8, wide), jnp.float32),
            pltpu.VMEM((HD, wide), jnp.float32),
            pltpu.VMEM((SIDE, 8, TOK), jnp.int32),
            pltpu.VMEM((SLOTS, 2, 2, TOK, HD), jnp.float32),
            pltpu.VMEM((SLOTS, HD, wide), jnp.bfloat16),
            pltpu.VMEM((SIDE,) + piece, jnp.bfloat16),
            pltpu.VMEM((2,) + piece, jnp.float32),
            pltpu.VMEM((SIDE, 3, TOK, 2 * HD), jnp.bfloat16),
            pltpu.VMEM((SIDE, 2, TOK, HD), jnp.bfloat16),
            pltpu.SemaphoreType.DMA((COPIES,)),
            pltpu.SemaphoreType.DMA((COPIES,)),
            pltpu.SemaphoreType.DMA((7,)),
        ],
        compiler_params=pltpu.CompilerParams(
            collective_id=0, has_side_effects=True, vmem_limit_bytes=VMEM_GRANT
        ),
        name="step",
    )(*arguments, doc_lengths)


def emit_kernel(a, b, c, out_a, out_b, out_c, sems):
    copies = [
        pltpu.make_async_copy(src, dst, sems.at[i])
        for i, (src, dst) in enumerate(((a, out_a), (b, out_b), (c, out_c)))
    ]
    for copy in copies:
        copy.start()
    for copy in copies:
        copy.wait()


def emit(*results):
    return pl.pallas_call(
        emit_kernel,
        out_shape=tuple(jax.ShapeDtypeStruct(r.shape, r.dtype) for r in results),
        in_specs=[pl.BlockSpec(memory_space=pl.ANY)] * 3,
        out_specs=(pl.BlockSpec(memory_space=pltpu.HBM),) * 3,
        scratch_shapes=[pltpu.SemaphoreType.DMA((3,))],
        compiler_params=pltpu.CompilerParams(vmem_limit_bytes=1024 * 1024),
        name="emit",
    )(*(pltpu.with_memory_space_constraint(r, pltpu.VMEM) for r in results))


def local(queries, keys, values, grad_out, doc_lengths):
    return emit(*one_step(queries, grad_out, keys, values, doc_lengths))


def solution(mesh):
    split = P(("dp", "seq"), None)
    return jax.shard_map(
        local,
        mesh=mesh,
        in_specs=(split, split, split, split, P()),
        out_specs=(split, split, split),
        check_vma=False,
    )
```

```python
import functools

import jax
import jax.numpy as jnp
from jax import lax
from jax.experimental import pallas as pl
from jax.experimental.pallas import tpu as pltpu
from jax.sharding import PartitionSpec as P

MESH = pl.DeviceIdType.MESH
SIDE = 4
TOK = 128
HD = 128
GW = 1024
PER_KV = GW // HD
GROUP = SIDE * SIDE * TOK
WIN = 2 * GROUP
KB = 256
SLOTS = 24
BEHIND = 15
EARLIEST = (0, 3, 8, 15)
FROM_X = (0, 1, 3, 2)
LOG2E = 1.4426950408889634
INV_ROOT = HD ** -0.5
LOW = -1e30
SCALE2 = INV_ROOT * LOG2E


def place():
    seq = lax.axis_index("seq")
    return lax.axis_index("dp"), lax.div(seq, SIDE), lax.rem(seq, SIDE)


def greet(dp, x, y):
    barrier = pltpu.get_barrier_semaphore()
    count = lax.axis_size("dp")
    peers = [{"seq": lax.rem(x + d, SIDE) * SIDE + y} for d in range(1, SIDE)]
    peers += [{"seq": x * SIDE + lax.rem(y + d, SIDE)} for d in range(1, SIDE)]
    peers += [{"dp": lax.rem(dp + 1, count)}, {"dp": lax.rem(dp + count - 1, count)}]
    for peer in peers:
        pl.semaphore_signal(barrier, inc=1, device_id=peer, device_id_type=MESH)
    pl.semaphore_wait(barrier, len(peers))


def cols(index, width):
    return pl.ds(pl.multiple_of(index * width, width), width)


def fold(tile):
    return tile.reshape(KB // 8, 8, HD)


def step_kernel(
    q, o, k, v, lens, out_q, out_k, out_v,
    land, kv, qs, os, s_buf, dp_buf, stats, run, final, dq, lows,
    terms, dqs, z_in, own, y_in, x_out, send, recv, here,
):
    dp, x, y = place()
    count = lax.axis_size("dp")
    used = [0]

    def remote(src, dst, device):
        i = used[0]
        used[0] += 1
        copy = pltpu.make_async_remote_copy(
            src_ref=src, dst_ref=dst, send_sem=send.at[i], recv_sem=recv.at[i],
            device_id=device, device_id_type=MESH,
        )
        copy.start()
        return copy

    def local_copy(src, dst, i):
        copy = pltpu.make_async_copy(src, dst, here.at[i])
        copy.start()
        return copy

    def at_x(d):
        return {"seq": lax.rem(x + d, SIDE) * SIDE + y}

    def at_y(d):
        return {"seq": x * SIDE + lax.rem(y + d, SIDE)}

    after = {"dp": lax.rem(dp + 1, count)}
    before = {"dp": lax.rem(dp + count - 1, count)}
    heads = [slice(h * HD, (h + 1) * HD) for h in range(PER_KV)]

    kv_here = [local_copy(a.at[:, cols(x, HD)], kv.at[n, 1, x, y], n) for n, a in enumerate((k, v))]
    q_here = [local_copy(a.at[:, cols(x, GW)], land.at[0, n], 2 + n) for n, a in enumerate((q, o))]
    greet(dp, x, y)
    first = []
    for d in (1, 3, 2):
        for n, a in enumerate((k, v)):
            head = lax.rem(x + d, SIDE)
            first.append(remote(a.at[:, cols(head, HD)], kv.at[n, 1, x, y], at_x(d)))
    arrive = {}
    for d in (3, 1, 2):
        slot = FROM_X.index(SIDE - d)
        head = lax.rem(x + d, SIDE)
        arrive[slot] = [
            remote(a.at[:, cols(head, GW)], land.at[slot, n], at_x(d)) for n, a in enumerate((q, o))
        ]

    def take(slot):
        for copy in q_here if slot == 0 else arrive[slot]:
            if slot == 0:
                copy.wait()
            else:
                copy.wait_recv()
        for h, span in enumerate(heads):
            qs[slot, span, :] = land[slot, 0, :, span]
            os[slot, span, :] = land[slot, 1, :, span]

    for copy in kv_here:
        copy.wait()
    for copy in first:
        copy.wait_recv()
    mine = kv.at[:, 1, :, y]
    along = [remote(mine, mine, at_y(d)) for d in (1, 3)]
    later = [remote(mine, kv.at[:, 0, :, y], after)]
    onward = []
    for copy, d in zip(along, (1, 3)):
        copy.wait_recv()
        source = lax.rem(y + SIDE - d, SIDE)
        part = kv.at[:, 1, pl.ds(d - 1 if d == 1 else 2, 2), source]
        onward.append(remote(part, part, at_y(d)))
        later.append(remote(kv.at[:, 1, :, source], kv.at[:, 0, :, source], after))
    take(0)
    run[...] = jnp.zeros_like(run)

    def at_least(value, bound):
        return (value >= bound).astype(jnp.int32)

    first_key = (dp - 1) * GROUP
    spots, steps, bases, blocks = [], [], [], []
    ready = jnp.int32(0)
    for slot in range(SIDE):
        block = lax.rem(x + FROM_X[slot], SIDE) * SIDE + y
        head_pos = dp * GROUP + block * TOK
        pos = head_pos + lax.broadcasted_iota(jnp.int32, (8, TOK), 1)

        def one_doc(i, state):
            end, low, low_row = state
            end = end + lens[i]
            low = jnp.maximum(low, end * at_least(head_pos, end))
            low_row = jnp.where(end <= pos, end, low_row)
            return end, low, low_row

        zero = jnp.int32(0)
        _, low, low_row = lax.fori_loop(
            0, lens.shape[0], one_doc, (zero, zero, jnp.zeros((8, TOK), jnp.int32))
        )
        lows[slot] = low_row - first_key
        end_block = GROUP // TOK + block + 1
        length = lax.div(end_block - lax.div(low - first_key, TOK) + 1, 2)
        spot = jnp.maximum(ready, EARLIEST[slot])
        ready = spot + length
        spots.append(spot)
        steps.append(length)
        bases.append(jnp.maximum(0, end_block - 2 * length))
        blocks.append(block)

    def pick(slot, values):
        picked = values[0]
        for n in range(1, SIDE):
            picked = picked + at_least(slot, n) * (values[n] - values[n - 1])
        return picked

    def step_of(i):
        slot = sum(at_least(i, spot) for spot in spots[1:])
        j = i - pick(slot, spots)
        lead = pick(slot, bases) + 2 * jnp.minimum(j, pick(slot, steps) - 1)
        return slot, j, jnp.minimum(lead, WIN // TOK - 2)

    def rows(n, lead):
        pieces = []
        for c in (lead, lead + 1):
            pieces.append(kv[n, lax.shift_right_logical(c, 4), lax.shift_right_logical(c, 2) & 3, c & 3])
        return jnp.concatenate(pieces, axis=0)

    nt = (((1,), (1,)), ((), ()))
    tn = (((0,), (0,)), ((), ()))
    nn = (((1,), (0,)), ((), ()))

    def dot(a, b, dims):
        return lax.dot_general(a, b, dims, preferred_element_type=jnp.float32)

    def score_step(i):
        slot, j, lead = step_of(i)
        scores = dot(rows(0, lead), qs[slot], nt)
        dprobs = dot(rows(1, lead), os[slot], nt)
        key = lead * TOK + lax.broadcasted_iota(jnp.int32, (KB, TOK), 0)
        last = GROUP + pick(slot, blocks) * TOK + lax.broadcasted_iota(jnp.int32, (KB, TOK), 1)
        new_block = jnp.broadcast_to(j, (8, HD)) == 0
        allowed = (key >= jnp.broadcast_to(lows[slot][0:1], (KB, TOK))) & (key <= last)
        for h, span in enumerate(heads):
            tile = jnp.where(allowed, scores[:, span] * SCALE2, LOW)
            s_buf[i, :, :, span] = tile.reshape(2, TOK, HD)
            dprob = dprobs[:, span]
            dprob = dprob.astype(jnp.bfloat16)
            dp_buf[i, :, span] = dprob
            dprob = dprob.astype(jnp.float32)
            old = jnp.where(new_block, LOW, run[0, :, span])
            new = jnp.maximum(old, jnp.max(fold(tile), axis=0))
            weight = jnp.exp2(fold(tile) - new[None])
            shrink = jnp.exp2(old - new)
            norm = jnp.where(new_block, 0.0, run[1, :, span])
            dots = jnp.where(new_block, 0.0, run[2, :, span])
            norm = norm * shrink + jnp.sum(weight, axis=0)
            dots = dots * shrink + jnp.sum(weight * fold(dprob), axis=0)
            for n, value in enumerate((new, norm, dots)):
                run[n, :, span] = value
                stats[i, n, :, span] = value

    for copy, d in zip(onward, (1, 3)):
        copy.wait_recv()
    far = lax.rem(y + 2, SIDE)
    later.append(remote(kv.at[:, 1, :, far], kv.at[:, 0, :, far], after))
    for copy in later:
        copy.wait_recv()
    for slot in range(SIDE):
        if slot:
            take(slot)
        pl.loop(EARLIEST[slot], (EARLIEST + (SLOTS,))[slot + 1])(score_step)

    for slot in range(SIDE):
        end = jnp.minimum(spots[slot] + steps[slot], SLOTS) - 1
        part = stats[end, 0]
        peak = jnp.max(part, axis=0, keepdims=True)
        share = jnp.exp2(part - peak)
        total = jnp.sum(stats[end, 1] * share, axis=0, keepdims=True)
        delta = jnp.sum(stats[end, 2] * share, axis=0, keepdims=True) / total
        final[slot, 0] = jnp.broadcast_to(peak + jnp.log2(total), part.shape)
        final[slot, 1] = jnp.broadcast_to(delta, part.shape)

    behind = [
        jnp.clip(lax.shift_right_arithmetic(17 - bases[slot], 1), 0, steps[slot])
        for slot in range(SIDE)
    ]
    counts = behind + [steps[slot] - behind[slot] for slot in range(SIDE)]
    opens = [jnp.int32(0)]
    for n in range(2 * SIDE - 1):
        opens.append(opens[-1] + counts[n])

    def pick_run(run, values):
        picked = values[0]
        for n in range(1, 2 * SIDE):
            picked = picked + at_least(run, n) * (values[n] - values[n - 1])
        return picked

    dq[...] = jnp.zeros_like(dq)

    def grad_step(t):
        part = sum(at_least(t, begin) for begin in opens[1:])
        slot = part & 3
        j = t - pick_run(part, opens)
        at = jnp.minimum(j + at_least(part, SIDE) * pick(slot, behind), pick(slot, steps) - 1)
        lead = jnp.minimum(pick(slot, bases) + 2 * at, WIN // TOK - 2)
        i = jnp.clip(pick(slot, spots) + at, 0, SLOTS - 1)
        probs, dscores = [], []
        for h, span in enumerate(heads):
            prob = jnp.exp2(fold(s_buf[i, :, :, span]) - final[slot, 0, :, span][None])
            dprob = fold(dp_buf[i, :, span].astype(jnp.float32))
            dscore = prob * (dprob - final[slot, 1, :, span][None])
            probs.append(prob.reshape(KB, TOK).astype(jnp.bfloat16))
            dscores.append(dscore.reshape(KB, TOK).astype(jnp.bfloat16))
        probs = jnp.concatenate(probs, axis=1)
        dscores = jnp.concatenate(dscores, axis=1)
        terms[t, 1] = dot(probs, os[slot], nn).reshape(2, TOK, HD)
        terms[t, 0] = dot(dscores, qs[slot], nn).reshape(2, TOK, HD)
        now = dq[...] * jnp.clip(j, 0, 1).astype(jnp.float32) + dot(rows(0, lead), dscores, tn)
        dq[...] = now
        dqs[t] = now.astype(jnp.bfloat16)

    def key_sum(c):
        sums = [jnp.zeros((TOK, HD), jnp.float32)] * 2
        for slot in range(SIDE):
            off = c - bases[slot]
            inside = (at_least(off, 0) * at_least(2 * steps[slot] - 1, off)).astype(jnp.float32)
            j = lax.shift_right_arithmetic(off, 1)
            own_part = at_least(j, behind[slot])
            t = j + opens[slot] + own_part * (opens[SIDE + slot] - opens[slot] - behind[slot])
            t = jnp.clip(t, 0, SLOTS - 1)
            for n in range(2):
                sums[n] += inside * terms[t, n, off & 1]
        return sums[0] * INV_ROOT, sums[1]

    order = (2, 1, 3, 0)
    pl.loop(0, BEHIND)(grad_step)
    down = {}

    def send_row(d):
        row = lax.rem(x + d, SIDE)

        @pl.loop(0, SIDE)
        def _(column):
            for n, total in enumerate(key_sum(row * SIDE + column)):
                kv[n, 0, row, column] = total.astype(jnp.bfloat16)

        if d:
            down[d] = [remote(kv.at[:, 0, row], z_in.at[d], before)]
        else:
            down[d] = []
            for e in order:
                column = lax.rem(y + e, SIDE)
                down[d].append(remote(kv.at[:, 0, row, column], z_in.at[d, :, column], before))
    for d in order[:2]:
        send_row(d)
    pl.loop(BEHIND, SLOTS)(grad_step)

    back_q = []
    for slot in (3, 1, 2, 0):
        if slot == 0:
            for d in order[2:]:
                send_row(d)
        ends = []
        for n in (slot, SIDE + slot):
            held = jnp.clip(opens[n] + counts[n] - 1, 0, SLOTS - 1)
            ends.append((held, at_least(counts[n], 1).astype(jnp.float32) * INV_ROOT))
        for h, span in enumerate(heads):
            block = sum(weight * dqs[held, :, span].astype(jnp.float32) for held, weight in ends)
            land[slot, 0, :, span] = block.T.astype(jnp.bfloat16)
        if slot:
            back_q.append(remote(land.at[slot, 0], out_q.at[:, cols(x, GW)], at_x(FROM_X[slot])))
    own_q = local_copy(land.at[0, 0], out_q.at[:, cols(x, GW)], 4)

    across, back = {}, []

    def finish(d):
        for e in (1, 2, 3):
            across[d][e].wait_recv()
        for n in range(2):
            rest = own[order.index(d) % 2, n, y]
            for e in (1, 2, 3):
                rest = rest + y_in[d, e - 1, :, n * HD:(n + 1) * HD].astype(jnp.float32)
            x_out[d, n] = rest.astype(jnp.bfloat16)
        if d:
            for n, out in enumerate((out_k, out_v)):
                back.append(remote(x_out.at[d, n], out.at[:, cols(x, HD)], at_x(d)))

    for n, d in enumerate(order):
        row, side = lax.rem(x + d, SIDE), n % 2

        @pl.loop(0, SIDE)
        def _(column):
            for n, total in enumerate(key_sum(GROUP // TOK + row * SIDE + column)):
                own[side, n, column] = total

        across[d] = {}
        for e in order:
            if d == 0 or e == order[0]:
                down[d][order.index(e) if d == 0 else 0].wait_recv()
            column = lax.rem(y + e, SIDE)
            whole = own[side, :, column] + z_in[d, :, column].astype(jnp.float32)
            if e:
                leave = slice((e - 1) * 2 * HD, e * 2 * HD)
                land[d, 1, :, leave] = jnp.concatenate([whole[0], whole[1]], axis=1).astype(jnp.bfloat16)
                across[d][e] = remote(land.at[d, 1, :, leave], y_in.at[d, e - 1], at_y(e))
            else:
                own[side, :, column] = whole
        if n:
            finish(order[n - 1])
    finish(order[-1])
    own_kv = [local_copy(x_out.at[0, n], out.at[:, cols(x, HD)], 5 + n) for n, out in enumerate((out_k, out_v))]
    for copy in back_q + back:
        copy.wait_recv()
    for copy in [own_q] + own_kv:
        copy.wait()
    gone = first + along + later + onward + back_q + back
    gone += [copy for copies in across.values() for copy in copies.values()]
    for copies in list(arrive.values()) + list(down.values()) + [gone]:
        for copy in copies:
            copy.wait_send()


VMEM_GRANT = 65536000
COPIES = 6 + 6 + 2 + 2 + 4 + 7 + 3 + 12 + 6


def one_step(queries, grad_out, keys, values, doc_lengths):
    piece = (2, SIDE, TOK, HD)
    wide = PER_KV * TOK
    hbm = pl.BlockSpec(memory_space=pltpu.HBM)
    arguments = [
        pltpu.with_memory_space_constraint(a, pltpu.HBM) for a in (queries, grad_out, keys, values)
    ]
    return pl.pallas_call(
        step_kernel,
        out_shape=(
            pltpu.VMEM((TOK, SIDE * GW), jnp.bfloat16),
            pltpu.VMEM((TOK, SIDE * HD), jnp.bfloat16),
            pltpu.VMEM((TOK, SIDE * HD), jnp.bfloat16),
        ),
        in_specs=[hbm] * 4 + [pl.BlockSpec(memory_space=pltpu.SMEM)],
        out_specs=(pl.BlockSpec(memory_space=pl.ANY),) * 3,
        scratch_shapes=[
            pltpu.VMEM((SIDE, 2, TOK, GW), jnp.bfloat16),
            pltpu.VMEM((2, 2, SIDE, SIDE, TOK, HD), jnp.bfloat16),
            pltpu.VMEM((SIDE, wide, HD), jnp.bfloat16),
            pltpu.VMEM((SIDE, wide, HD), jnp.bfloat16),
            pltpu.VMEM((SLOTS, 2, TOK, wide), jnp.float32),
            pltpu.VMEM((SLOTS, KB, wide), jnp.bfloat16),
            pltpu.VMEM((SLOTS, 3, 8, wide), jnp.float32),
            pltpu.VMEM((3, 8, wide), jnp.float32),
            pltpu.VMEM((SIDE, 2, 8, wide), jnp.float32),
            pltpu.VMEM((HD, wide), jnp.float32),
            pltpu.VMEM((SIDE, 8, TOK), jnp.int32),
            pltpu.VMEM((SLOTS, 2, 2, TOK, HD), jnp.float32),
            pltpu.VMEM((SLOTS, HD, wide), jnp.bfloat16),
            pltpu.VMEM((SIDE,) + piece, jnp.bfloat16),
            pltpu.VMEM((2,) + piece, jnp.float32),
            pltpu.VMEM((SIDE, 3, TOK, 2 * HD), jnp.bfloat16),
            pltpu.VMEM((SIDE, 2, TOK, HD), jnp.bfloat16),
            pltpu.SemaphoreType.DMA((COPIES,)),
            pltpu.SemaphoreType.DMA((COPIES,)),
            pltpu.SemaphoreType.DMA((7,)),
        ],
        compiler_params=pltpu.CompilerParams(
            collective_id=0, has_side_effects=True, vmem_limit_bytes=VMEM_GRANT
        ),
        name="step",
    )(*arguments, doc_lengths)


def emit_kernel(a, b, c, out_a, out_b, out_c, sems):
    copies = [
        pltpu.make_async_copy(src, dst, sems.at[i])
        for i, (src, dst) in enumerate(((a, out_a), (b, out_b), (c, out_c)))
    ]
    for copy in copies:
        copy.start()
    for copy in copies:
        copy.wait()


def emit(*results):
    return pl.pallas_call(
        emit_kernel,
        out_shape=tuple(jax.ShapeDtypeStruct(r.shape, r.dtype) for r in results),
        in_specs=[pl.BlockSpec(memory_space=pl.ANY)] * 3,
        out_specs=(pl.BlockSpec(memory_space=pltpu.HBM),) * 3,
        scratch_shapes=[pltpu.SemaphoreType.DMA((3,))],
        compiler_params=pltpu.CompilerParams(vmem_limit_bytes=1024 * 1024),
        name="emit",
    )(*(pltpu.with_memory_space_constraint(r, pltpu.VMEM) for r in results))


def local(queries, keys, values, grad_out, doc_lengths):
    return emit(*one_step(queries, grad_out, keys, values, doc_lengths))


def solution(mesh):
    split = P(("dp", "seq"), None)
    return jax.shard_map(
        local,
        mesh=mesh,
        in_specs=(split, split, split, split, P()),
        out_specs=(split, split, split),
        check_vma=False,
    )
```

```python
import functools

import jax
import jax.numpy as jnp
from jax import lax
from jax.experimental import pallas as pl
from jax.experimental.pallas import tpu as pltpu
from jax.sharding import PartitionSpec as P

MESH = pl.DeviceIdType.MESH
SIDE = 4
TOK = 128
HD = 128
GW = 1024
PER_KV = GW // HD
GROUP = SIDE * SIDE * TOK
WIN = 2 * GROUP
KB = 256
SLOTS = 24
BEHIND = 15
EARLIEST = (0, 3, 8, 15)
FROM_X = (0, 1, 3, 2)
LOG2E = 1.4426950408889634
INV_ROOT = HD ** -0.5
LOW = -1e30
SCALE2 = INV_ROOT * LOG2E


def place():
    seq = lax.axis_index("seq")
    return lax.axis_index("dp"), lax.div(seq, SIDE), lax.rem(seq, SIDE)


def greet(dp, x, y):
    barrier = pltpu.get_barrier_semaphore()
    count = lax.axis_size("dp")
    peers = [{"seq": lax.rem(x + d, SIDE) * SIDE + y} for d in range(1, SIDE)]
    peers += [{"seq": x * SIDE + lax.rem(y + d, SIDE)} for d in range(1, SIDE)]
    peers += [{"dp": lax.rem(dp + 1, count)}, {"dp": lax.rem(dp + count - 1, count)}]
    for peer in peers:
        pl.semaphore_signal(barrier, inc=1, device_id=peer, device_id_type=MESH)
    pl.semaphore_wait(barrier, len(peers))


def cols(index, width):
    return pl.ds(pl.multiple_of(index * width, width), width)


def fold(tile):
    return tile.reshape(KB // 8, 8, HD)


def step_kernel(
    q, o, k, v, lens, out_q, out_k, out_v,
    land, kv, qs, os, s_buf, dp_buf, stats, run, final, dq, lows,
    terms, dqs, z_in, own, y_in, x_out, send, recv, here,
):
    dp, x, y = place()
    count = lax.axis_size("dp")
    used = [0]

    def remote(src, dst, device):
        i = used[0]
        used[0] += 1
        copy = pltpu.make_async_remote_copy(
            src_ref=src, dst_ref=dst, send_sem=send.at[i], recv_sem=recv.at[i],
            device_id=device, device_id_type=MESH,
        )
        copy.start()
        return copy

    def local_copy(src, dst, i):
        copy = pltpu.make_async_copy(src, dst, here.at[i])
        copy.start()
        return copy

    def at_x(d):
        return {"seq": lax.rem(x + d, SIDE) * SIDE + y}

    def at_y(d):
        return {"seq": x * SIDE + lax.rem(y + d, SIDE)}

    after = {"dp": lax.rem(dp + 1, count)}
    before = {"dp": lax.rem(dp + count - 1, count)}
    heads = [slice(h * HD, (h + 1) * HD) for h in range(PER_KV)]

    kv_here = [local_copy(a.at[:, cols(x, HD)], kv.at[n, 1, x, y], n) for n, a in enumerate((k, v))]
    q_here = [local_copy(a.at[:, cols(x, GW)], land.at[0, n], 2 + n) for n, a in enumerate((q, o))]
    greet(dp, x, y)
    first = []
    for d in (1, 3, 2):
        for n, a in enumerate((k, v)):
            head = lax.rem(x + d, SIDE)
            first.append(remote(a.at[:, cols(head, HD)], kv.at[n, 1, x, y], at_x(d)))
    arrive = {}
    for d in (3, 1, 2):
        slot = FROM_X.index(SIDE - d)
        head = lax.rem(x + d, SIDE)
        arrive[slot] = [
            remote(a.at[:, cols(head, GW)], land.at[slot, n], at_x(d)) for n, a in enumerate((q, o))
        ]

    def take(slot):
        for copy in q_here if slot == 0 else arrive[slot]:
            if slot == 0:
                copy.wait()
            else:
                copy.wait_recv()
        for h, span in enumerate(heads):
            qs[slot, span, :] = land[slot, 0, :, span]
            os[slot, span, :] = land[slot, 1, :, span]

    for copy in kv_here:
        copy.wait()
    for copy in first:
        copy.wait_recv()
    mine = kv.at[:, 1, :, y]
    along = [remote(mine, mine, at_y(d)) for d in (1, 3)]
    later = [remote(mine, kv.at[:, 0, :, y], after)]
    onward = []
    for copy, d in zip(along, (1, 3)):
        copy.wait_recv()
        source = lax.rem(y + SIDE - d, SIDE)
        part = kv.at[:, 1, pl.ds(d - 1 if d == 1 else 2, 2), source]
        onward.append(remote(part, part, at_y(d)))
        later.append(remote(kv.at[:, 1, :, source], kv.at[:, 0, :, source], after))
    take(0)
    run[...] = jnp.zeros_like(run)

    def at_least(value, bound):
        return (value >= bound).astype(jnp.int32)

    first_key = (dp - 1) * GROUP
    spots, steps, bases, blocks = [], [], [], []
    ready = jnp.int32(0)
    for slot in range(SIDE):
        block = lax.rem(x + FROM_X[slot], SIDE) * SIDE + y
        head_pos = dp * GROUP + block * TOK
        pos = head_pos + lax.broadcasted_iota(jnp.int32, (8, TOK), 1)

        def one_doc(i, state):
            end, low, low_row = state
            end = end + lens[i]
            low = jnp.maximum(low, end * at_least(head_pos, end))
            low_row = jnp.where(end <= pos, end, low_row)
            return end, low, low_row

        zero = jnp.int32(0)
        _, low, low_row = lax.fori_loop(
            0, lens.shape[0], one_doc, (zero, zero, jnp.zeros((8, TOK), jnp.int32))
        )
        lows[slot] = low_row - first_key
        end_block = GROUP // TOK + block + 1
        length = lax.div(end_block - lax.div(low - first_key, TOK) + 1, 2)
        spot = jnp.maximum(ready, EARLIEST[slot])
        ready = spot + length
        spots.append(spot)
        steps.append(length)
        bases.append(jnp.maximum(0, end_block - 2 * length))
        blocks.append(block)

    def pick(slot, values):
        picked = values[0]
        for n in range(1, SIDE):
            picked = picked + at_least(slot, n) * (values[n] - values[n - 1])
        return picked

    def step_of(i):
        slot = sum(at_least(i, spot) for spot in spots[1:])
        j = i - pick(slot, spots)
        lead = pick(slot, bases) + 2 * jnp.minimum(j, pick(slot, steps) - 1)
        return slot, j, jnp.minimum(lead, WIN // TOK - 2)

    def rows(n, lead):
        pieces = []
        for c in (lead, lead + 1):
            pieces.append(kv[n, lax.shift_right_logical(c, 4), lax.shift_right_logical(c, 2) & 3, c & 3])
        return jnp.concatenate(pieces, axis=0)

    nt = (((1,), (1,)), ((), ()))
    tn = (((0,), (0,)), ((), ()))
    nn = (((1,), (0,)), ((), ()))

    def dot(a, b, dims):
        return lax.dot_general(a, b, dims, preferred_element_type=jnp.float32)

    def score_step(i):
        slot, j, lead = step_of(i)
        scores = dot(rows(0, lead), qs[slot], nt)
        dprobs = dot(rows(1, lead), os[slot], nt)
        key = lead * TOK + lax.broadcasted_iota(jnp.int32, (KB, TOK), 0)
        last = GROUP + pick(slot, blocks) * TOK + lax.broadcasted_iota(jnp.int32, (KB, TOK), 1)
        new_block = jnp.broadcast_to(j, (8, HD)) == 0
        allowed = (key >= jnp.broadcast_to(lows[slot][0:1], (KB, TOK))) & (key <= last)
        for h, span in enumerate(heads):
            tile = jnp.where(allowed, scores[:, span] * SCALE2, LOW)
            s_buf[i, :, :, span] = tile.reshape(2, TOK, HD)
            dprob = dprobs[:, span]
            dprob = dprob.astype(jnp.bfloat16)
            dp_buf[i, :, span] = dprob
            dprob = dprob.astype(jnp.float32)
            old = jnp.where(new_block, LOW, run[0, :, span])
            new = jnp.maximum(old, jnp.max(fold(tile), axis=0))
            weight = jnp.exp2(fold(tile) - new[None])
            shrink = jnp.exp2(old - new)
            norm = jnp.where(new_block, 0.0, run[1, :, span])
            dots = jnp.where(new_block, 0.0, run[2, :, span])
            norm = norm * shrink + jnp.sum(weight, axis=0)
            dots = dots * shrink + jnp.sum(weight * fold(dprob), axis=0)
            for n, value in enumerate((new, norm, dots)):
                run[n, :, span] = value
                stats[i, n, :, span] = value

    for copy, d in zip(onward, (1, 3)):
        copy.wait_recv()
    far = lax.rem(y + 2, SIDE)
    later.append(remote(kv.at[:, 1, :, far], kv.at[:, 0, :, far], after))
    for copy in later:
        copy.wait_recv()
    for slot in range(SIDE):
        if slot:
            take(slot)
        pl.loop(EARLIEST[slot], (EARLIEST + (SLOTS,))[slot + 1])(score_step)

    for slot in range(SIDE):
        end = jnp.minimum(spots[slot] + steps[slot], SLOTS) - 1
        part = stats[end, 0]
        peak = jnp.max(part, axis=0, keepdims=True)
        share = jnp.exp2(part - peak)
        total = jnp.sum(stats[end, 1] * share, axis=0, keepdims=True)
        delta = jnp.sum(stats[end, 2] * share, axis=0, keepdims=True) / total
        final[slot, 0] = jnp.broadcast_to(peak + jnp.log2(total), part.shape)
        final[slot, 1] = jnp.broadcast_to(delta, part.shape)

    behind = [
        jnp.clip(lax.shift_right_arithmetic(17 - bases[slot], 1), 0, steps[slot])
        for slot in range(SIDE)
    ]
    counts = behind + [steps[slot] - behind[slot] for slot in range(SIDE)]
    opens = [jnp.int32(0)]
    for n in range(2 * SIDE - 1):
        opens.append(opens[-1] + counts[n])

    def pick_run(run, values):
        picked = values[0]
        for n in range(1, 2 * SIDE):
            picked = picked + at_least(run, n) * (values[n] - values[n - 1])
        return picked

    dq[...] = jnp.zeros_like(dq)

    def grad_step(t):
        part = sum(at_least(t, begin) for begin in opens[1:])
        slot = part & 3
        j = t - pick_run(part, opens)
        at = jnp.minimum(j + at_least(part, SIDE) * pick(slot, behind), pick(slot, steps) - 1)
        lead = jnp.minimum(pick(slot, bases) + 2 * at, WIN // TOK - 2)
        i = jnp.clip(pick(slot, spots) + at, 0, SLOTS - 1)
        probs, dscores = [], []
        for h, span in enumerate(heads):
            prob = jnp.exp2(fold(s_buf[i, :, :, span]) - final[slot, 0, :, span][None])
            dprob = fold(dp_buf[i, :, span].astype(jnp.float32))
            dscore = prob * (dprob - final[slot, 1, :, span][None])
            probs.append(prob.reshape(KB, TOK).astype(jnp.bfloat16))
            dscores.append(dscore.reshape(KB, TOK).astype(jnp.bfloat16))
        probs = jnp.concatenate(probs, axis=1)
        dscores = jnp.concatenate(dscores, axis=1)
        terms[t, 1] = dot(probs, os[slot], nn).reshape(2, TOK, HD)
        terms[t, 0] = dot(dscores, qs[slot], nn).reshape(2, TOK, HD)
        now = dq[...] * jnp.clip(j, 0, 1).astype(jnp.float32) + dot(rows(0, lead), dscores, tn)
        dq[...] = now
        dqs[t] = (now * INV_ROOT).astype(jnp.bfloat16)

    def key_sum(c):
        sums = [jnp.zeros((TOK, HD), jnp.float32)] * 2
        for slot in range(SIDE):
            off = c - bases[slot]
            inside = (at_least(off, 0) * at_least(2 * steps[slot] - 1, off)).astype(jnp.float32)
            j = lax.shift_right_arithmetic(off, 1)
            own_part = at_least(j, behind[slot])
            t = j + opens[slot] + own_part * (opens[SIDE + slot] - opens[slot] - behind[slot])
            t = jnp.clip(t, 0, SLOTS - 1)
            for n in range(2):
                sums[n] += inside * terms[t, n, off & 1]
        return sums[0] * INV_ROOT, sums[1]

    order = (2, 1, 3, 0)
    pl.loop(0, BEHIND)(grad_step)
    down = {}
    for d in order:
        row = lax.rem(x + d, SIDE)

        @pl.loop(0, SIDE)
        def _(column):
            for n, total in enumerate(key_sum(row * SIDE + column)):
                kv[n, 0, row, column] = total.astype(jnp.bfloat16)

        if d:
            down[d] = [remote(kv.at[:, 0, row], z_in.at[d], before)]
        else:
            down[d] = []
            for e in order:
                column = lax.rem(y + e, SIDE)
                down[d].append(remote(kv.at[:, 0, row, column], z_in.at[d, :, column], before))
    pl.loop(BEHIND, SLOTS)(grad_step)

    back_q = []
    for slot in (3, 1, 2, 0):
        ends = []
        for n in (slot, SIDE + slot):
            held = jnp.clip(opens[n] + counts[n] - 1, 0, SLOTS - 1)
            ends.append((held, at_least(counts[n], 1).astype(jnp.float32)))
        for h, span in enumerate(heads):
            block = sum(weight * dqs[held, :, span].astype(jnp.float32) for held, weight in ends)
            land[slot, 0, :, span] = block.T.astype(jnp.bfloat16)
        if slot:
            back_q.append(remote(land.at[slot, 0], out_q.at[:, cols(x, GW)], at_x(FROM_X[slot])))
    own_q = local_copy(land.at[0, 0], out_q.at[:, cols(x, GW)], 4)

    across, back = {}, []

    def finish(d):
        for e in (1, 2, 3):
            across[d][e].wait_recv()
        for n in range(2):
            rest = own[order.index(d) % 2, n, y]
            for e in (1, 2, 3):
                rest = rest + y_in[d, e - 1, :, n * HD:(n + 1) * HD].astype(jnp.float32)
            x_out[d, n] = rest.astype(jnp.bfloat16)
        if d:
            for n, out in enumerate((out_k, out_v)):
                back.append(remote(x_out.at[d, n], out.at[:, cols(x, HD)], at_x(d)))

    for n, d in enumerate(order):
        row, side = lax.rem(x + d, SIDE), n % 2

        @pl.loop(0, SIDE)
        def _(column):
            for n, total in enumerate(key_sum(GROUP // TOK + row * SIDE + column)):
                own[side, n, column] = total

        across[d] = {}
        for e in order:
            if d == 0 or e == order[0]:
                down[d][order.index(e) if d == 0 else 0].wait_recv()
            column = lax.rem(y + e, SIDE)
            whole = own[side, :, column] + z_in[d, :, column].astype(jnp.float32)
            if e:
                leave = slice((e - 1) * 2 * HD, e * 2 * HD)
                land[d, 1, :, leave] = jnp.concatenate([whole[0], whole[1]], axis=1).astype(jnp.bfloat16)
                across[d][e] = remote(land.at[d, 1, :, leave], y_in.at[d, e - 1], at_y(e))
            else:
                own[side, :, column] = whole
        if n:
            finish(order[n - 1])
    finish(order[-1])
    own_kv = [local_copy(x_out.at[0, n], out.at[:, cols(x, HD)], 5 + n) for n, out in enumerate((out_k, out_v))]
    for copy in back_q + back:
        copy.wait_recv()
    for copy in [own_q] + own_kv:
        copy.wait()
    gone = first + along + later + onward + back_q + back
    gone += [copy for copies in across.values() for copy in copies.values()]
    for copies in list(arrive.values()) + list(down.values()) + [gone]:
        for copy in copies:
            copy.wait_send()


VMEM_GRANT = 65536000
COPIES = 6 + 6 + 2 + 2 + 4 + 7 + 3 + 12 + 6


def one_step(queries, grad_out, keys, values, doc_lengths):
    piece = (2, SIDE, TOK, HD)
    wide = PER_KV * TOK
    hbm = pl.BlockSpec(memory_space=pltpu.HBM)
    arguments = [
        pltpu.with_memory_space_constraint(a, pltpu.HBM) for a in (queries, grad_out, keys, values)
    ]
    return pl.pallas_call(
        step_kernel,
        out_shape=(
            pltpu.VMEM((TOK, SIDE * GW), jnp.bfloat16),
            pltpu.VMEM((TOK, SIDE * HD), jnp.bfloat16),
            pltpu.VMEM((TOK, SIDE * HD), jnp.bfloat16),
        ),
        in_specs=[hbm] * 4 + [pl.BlockSpec(memory_space=pltpu.SMEM)],
        out_specs=(pl.BlockSpec(memory_space=pl.ANY),) * 3,
        scratch_shapes=[
            pltpu.VMEM((SIDE, 2, TOK, GW), jnp.bfloat16),
            pltpu.VMEM((2, 2, SIDE, SIDE, TOK, HD), jnp.bfloat16),
            pltpu.VMEM((SIDE, wide, HD), jnp.bfloat16),
            pltpu.VMEM((SIDE, wide, HD), jnp.bfloat16),
            pltpu.VMEM((SLOTS, 2, TOK, wide), jnp.float32),
            pltpu.VMEM((SLOTS, KB, wide), jnp.bfloat16),
            pltpu.VMEM((SLOTS, 3, 8, wide), jnp.float32),
            pltpu.VMEM((3, 8, wide), jnp.float32),
            pltpu.VMEM((SIDE, 2, 8, wide), jnp.float32),
            pltpu.VMEM((HD, wide), jnp.float32),
            pltpu.VMEM((SIDE, 8, TOK), jnp.int32),
            pltpu.VMEM((SLOTS, 2, 2, TOK, HD), jnp.float32),
            pltpu.VMEM((SLOTS, HD, wide), jnp.bfloat16),
            pltpu.VMEM((SIDE,) + piece, jnp.bfloat16),
            pltpu.VMEM((2,) + piece, jnp.float32),
            pltpu.VMEM((SIDE, 3, TOK, 2 * HD), jnp.bfloat16),
            pltpu.VMEM((SIDE, 2, TOK, HD), jnp.bfloat16),
            pltpu.SemaphoreType.DMA((COPIES,)),
            pltpu.SemaphoreType.DMA((COPIES,)),
            pltpu.SemaphoreType.DMA((7,)),
        ],
        compiler_params=pltpu.CompilerParams(
            collective_id=0, has_side_effects=True, vmem_limit_bytes=VMEM_GRANT
        ),
        name="step",
    )(*arguments, doc_lengths)


def emit_kernel(a, b, c, out_a, out_b, out_c, sems):
    copies = [
        pltpu.make_async_copy(src, dst, sems.at[i])
        for i, (src, dst) in enumerate(((a, out_a), (b, out_b), (c, out_c)))
    ]
    for copy in copies:
        copy.start()
    for copy in copies:
        copy.wait()


def emit(*results):
    return pl.pallas_call(
        emit_kernel,
        out_shape=tuple(jax.ShapeDtypeStruct(r.shape, r.dtype) for r in results),
        in_specs=[pl.BlockSpec(memory_space=pl.ANY)] * 3,
        out_specs=(pl.BlockSpec(memory_space=pltpu.HBM),) * 3,
        scratch_shapes=[pltpu.SemaphoreType.DMA((3,))],
        compiler_params=pltpu.CompilerParams(vmem_limit_bytes=1024 * 1024),
        name="emit",
    )(*(pltpu.with_memory_space_constraint(r, pltpu.VMEM) for r in results))


def local(queries, keys, values, grad_out, doc_lengths):
    return emit(*one_step(queries, grad_out, keys, values, doc_lengths))


def solution(mesh):
    split = P(("dp", "seq"), None)
    return jax.shard_map(
        local,
        mesh=mesh,
        in_specs=(split, split, split, split, P()),
        out_specs=(split, split, split),
        check_vma=False,
    )
```
